512 devices in a mesh: dp: 64 (over y, z_hi, core), tensor: 8 (over x, z_lo).
Axes of the slice: x: 4, y: 8, z: 8 (z_hi: 4, z_lo: 2; z = z_hi * 2 + z_lo), core: 2. Of those that a mesh axis runs over, the one named last changes fastest.
Arguments:
- inputs: float32 [16384, 1024], P('dp', 'tensor'), may hold values from -16 to 16
- cotangent: float32 [16384, 1024], P('dp', 'tensor'), may hold values from -0.12 to 0.12
- gate_weight: float32 [1024, 4096], P('dp', 'tensor'), may hold values from -0.1875 to 0.1875
- up_weight: float32 [1024, 4096], P('dp', 'tensor'), may hold values from -0.1875 to 0.1875
- down_weight: float32 [1024, 4096], P('dp', 'tensor'), may hold values from -0.09375 to 0.09375
- gate_first: float32 [1024, 4096], P('dp', 'tensor'), may hold values from -6 to 6
- gate_second: float32 [1024, 4096], P('dp', 'tensor'), may hold values from 0.5 to 4
- up_first: float32 [1024, 4096], P('dp', 'tensor'), may hold values from -6 to 6
- up_second: float32 [1024, 4096], P('dp', 'tensor'), may hold values from 0.5 to 4
Outputs:
- gate_new: float32 [1024, 4096], P('dp', 'tensor')
- gate_first_new: float32 [1024, 4096], P('dp', 'tensor')
- gate_second_new: float32 [1024, 4096], P('dp', 'tensor')
- up_new: float32 [1024, 4096], P('dp', 'tensor')
- up_first_new: float32 [1024, 4096], P('dp', 'tensor')
- up_second_new: float32 [1024, 4096], P('dp', 'tensor')
The draws below stay inside these ranges and needn't reach their ends.
All inputs are finite; a program needn't handle non-finite values.
Results may differ from the reference program's by a relative error of at most 0.00005.
Values sent between devices are 32-bit elements; how exact they have to be, the bound alone decides.
A program may use at most 64 MiB of HBM per device.

```python
import math
import jax
import jax.numpy as jnp
from jax import lax

D = 1024
FF = 4096
STEP = 100
TOKENS = 16384
N_TENSOR = 8


def raised(entries, own_key, source, target, shards_of, factor):
    def block_of(axis_at):
        return (jnp.arange(entries.shape[axis_at]) // (entries.shape[axis_at] // shards_of)).reshape((-1,) + (1,) * (entries.ndim - 1 - axis_at))

    first = jax.random.permutation(own_key, shards_of)[block_of(target)]
    far = (block_of(target) + shards_of // 2) % shards_of
    return jnp.where((block_of(source) == first) | (block_of(source) == far), factor * entries, entries)


def block_levels(rng, shape, shards, low, top_value):
    factor_of, own = 1.0, jax.random.fold_in(rng, 6)
    for axis_at, blocks in shards:
        steps = jnp.exp(jax.random.uniform(jax.random.fold_in(own, axis_at), (blocks,), jnp.float32, low / len(shards), top_value / len(shards)))
        factor_of = factor_of * jnp.repeat(steps, shape[axis_at] // blocks).reshape([-1 if axis == axis_at else 1 for axis in range(len(shape))])
    return factor_of


def gaussian(own_key, shape, scale, bound, shards=(), dtype=jnp.bfloat16):
    level = block_levels(own_key, shape, shards, -0.22, 0.18) if shards else 1.0
    values = jax.random.normal(own_key, shape, jnp.float32) * scale * level
    return jnp.minimum(jnp.maximum(values, -bound), bound).astype(dtype)


def gaussian_with(rng, extent, scale, bound, cuts, heavy, held_as=jnp.bfloat16):
    array = scale * jax.random.normal(rng, extent, jnp.float32)
    if cuts:
        array = array * block_levels(rng, extent, cuts, -0.22, 0.18)
    return jnp.clip(raised(array, jax.random.fold_in(rng, 3), *heavy), -bound, bound).astype(held_as)


def setup_inputs(seed: int = 0) -> dict:
    keys = jax.random.split(jax.random.key(seed), 10)
    return {
        "inputs": gaussian_with(keys[0], (TOKENS, D), 1.0, 16.0, ((0, 64), (1, 8)), (0, 1, 64, 4.0), jnp.float32),
        "cotangent": gaussian(keys[1], (TOKENS, D), 0.02, 0.12, ((0, 64), (1, 8)), jnp.float32),
        "gate_weight": gaussian(keys[2], (D, FF), D ** -0.5, 0.1875, ((0, 64), (1, 8)), jnp.float32),
        "up_weight": gaussian(keys[3], (D, FF), D ** -0.5, 0.1875, ((0, 64), (1, 8)), jnp.float32),
        "down_weight": gaussian(keys[4], (D, FF), FF ** -0.5, 0.09375, ((0, 64), (1, 8)), jnp.float32),
        "gate_first": gaussian(keys[5], (D, FF), 1.0, 6.0, ((0, 64), (1, 8)), jnp.float32),
        "gate_second": jnp.clip(jnp.exp(math.log(4.0) - 2.0794415 * jax.random.uniform(keys[6], (D, FF), jnp.float32) ** block_levels(keys[6], (D, FF), ((0, 64), (1, 8)), -0.2, 0.2)), 0.5, 4.0),
        "up_first": gaussian(keys[7], (D, FF), 1.0, 6.0, ((0, 64), (1, 8)), jnp.float32),
        "up_second": jnp.clip(jnp.exp(math.log(4.0) - 2.0794415 * jax.random.uniform(keys[8], (D, FF), jnp.float32) ** block_levels(keys[8], (D, FF), ((0, 64), (1, 8)), -0.2, 0.2)), 0.5, 4.0),
    }


def adam_update(weight, first, second, grad):
    first_new = 0.9 * first + 0.1 * grad
    second_new = 0.95 * second + 0.05 * grad * grad
    first_hat = first_new / (1.0 - 0.9 ** STEP)
    second_hat = second_new / (1.0 - 0.95 ** STEP)
    weight_new = weight - 0.003 * first_hat / (jnp.sqrt(second_hat) + 1e-08)
    return (weight_new, first_new, second_new)

def reference(inputs, cotangent, gate_weight, up_weight, down_weight, gate_first, gate_second, up_first, up_second):
    highest = lax.Precision.HIGHEST
    block_count = N_TENSOR
    block_width = FF // block_count

    def split_cols(weight):
        return jnp.transpose(weight.reshape(D, block_count, block_width), (1, 0, 2))

    def one_block(blocks):
        gate_part, lift_part, down_part = blocks
        gate_sum = jnp.dot(inputs, gate_part, precision=highest, preferred_element_type=jnp.float32)
        lift_sum = jnp.dot(inputs, lift_part, precision=highest, preferred_element_type=jnp.float32)
        back_sum = jnp.dot(cotangent, down_part, precision=highest, preferred_element_type=jnp.float32)
        sigmoid_gate = jax.nn.sigmoid(gate_sum)
        gate_rows = back_sum * lift_sum * sigmoid_gate * (1.0 + gate_sum * (1.0 - sigmoid_gate))
        lift_rows = back_sum * gate_sum * sigmoid_gate
        dims = (((0,), (0,)), ((), ()))
        gate_grad = lax.dot_general(inputs, gate_rows, dims, precision=highest, preferred_element_type=jnp.float32)
        lift_grad = lax.dot_general(inputs, lift_rows, dims, precision=highest, preferred_element_type=jnp.float32)
        return (gate_grad, lift_grad)
    gate_blocks, lift_blocks = lax.map(one_block, (split_cols(gate_weight), split_cols(up_weight), split_cols(down_weight)))
    gate_grad = jnp.transpose(gate_blocks, (1, 0, 2)).reshape(D, FF)
    lift_grad = jnp.transpose(lift_blocks, (1, 0, 2)).reshape(D, FF)
    gate_new, gate_first_new, gate_second_new = adam_update(gate_weight, gate_first, gate_second, gate_grad)
    up_new, up_first_new, up_second_new = adam_update(up_weight, up_first, up_second, lift_grad)
    return (gate_new, gate_first_new, gate_second_new, up_new, up_first_new, up_second_new)
```

```python
import jax
import jax.numpy as jnp
from jax import lax
from jax.experimental import pallas as pl
from jax.experimental.pallas import tpu as pltpu
from jax.sharding import PartitionSpec as P

STEP = 100
MESH = pl.DeviceIdType.MESH
F32 = jnp.float32
BF16 = jnp.bfloat16
NX, NZL, NY, NZH = 4, 2, 8, 4


def adam_update(weight, first, second, grad):
    first_new = 0.9 * first + 0.1 * grad
    second_new = 0.95 * second + 0.05 * grad * grad
    first_hat = first_new / (1.0 - 0.9**STEP)
    second_hat = second_new / (1.0 - 0.95**STEP)
    weight_new = weight - 0.003 * first_hat / (jnp.sqrt(second_hat) + 1e-08)
    return (weight_new, first_new, second_new)


def split(v):
    hi = v.astype(BF16)
    return hi, (v - hi.astype(F32)).astype(BF16)


def dot(a, b):
    return jnp.dot(a, b, preferred_element_type=F32)


def dot3(ah, al, bh, bl):
    return dot(ah, bh) + dot(ah, bl) + dot(al, bh)


def kernel(
    in_ref, cot_ref, gw_ref, uw_ref, dw_ref, out_ref,
    xc, w, xh, xl, ch, cl, xth, xtl, wh, wl, acc, rh, rl, gbuf, rbuf, tbuf, zbuf,
    own_sem, a_recv, a_send, s_recv, s_send, w_recv, w_send, y_recv, y_send,
    r_recv, r_send, z_recv, z_send,
):
    dp = lax.axis_index("dp")
    t = lax.axis_index("tensor")
    c = lax.rem(dp, 2)
    zh = lax.rem(dp // 2, NZH)
    y = dp // (2 * NZH)
    x = t // NZL
    zl = lax.rem(t, NZL)

    def t_of(dx, dz):
        zz = zl if dz == 0 else 1 - zl
        return lax.rem(x + dx, NX) * NZL + zz

    def y_of(d):
        return lax.rem(y + d, NY)

    def dp_of(yy, zz, cc):
        return (yy * NZH + zz) * 2 + cc

    sib = (dp_of(y, zh, 1 - c), t)
    zpart = (dp, t_of(0, 1))
    xr = (dp, t_of(1, 0))
    xleft = (dp, t_of(3, 0))
    yr = (dp_of(y_of(1), zh, c), t)
    yl = (dp_of(y_of(7), zh, c), t)

    def zc_of(dz, dc):
        zz = lax.rem(zh + dz, NZH)
        cc = c if dc == 0 else 1 - c
        return zz, cc, (dp_of(y, zz, cc), t)

    zpeers = [(dz, dc) for dz in range(NZH) for dc in range(2) if (dz, dc) != (0, 0)]

    barrier = pltpu.get_barrier_semaphore()
    peers = [zc_of(dz, dc)[2] for dz, dc in zpeers] + [zpart, xr, xleft, yr, yl]
    for peer in peers:
        pl.semaphore_signal(barrier, inc=1, device_id=peer, device_id_type=MESH)
    pl.semaphore_wait(barrier, len(peers))

    def remote(src, dst, send, recv, dev):
        pltpu.make_async_remote_copy(
            src_ref=src, dst_ref=dst, send_sem=send, recv_sem=recv,
            device_id=dev, device_id_type=MESH,
        ).start()

    def wait(ref, sem):
        pltpu.make_async_copy(ref, ref, sem).wait()

    w_srcs = (dw_ref, gw_ref, uw_ref)

    def w_first(k):
        row = pl.multiple_of(zh * 32 + c * 16, 16)
        for dz, dc in [(1, 0), (1, 1), (3, 0), (3, 1), (2, 0), (2, 1), (0, 1)]:
            _, cc, dev = zc_of(dz, dc)
            col = pl.multiple_of(cc * 256, 256)
            remote(
                w_srcs[k].at[:, pl.ds(col, 256)],
                w.at[y, k, pl.ds(row, 16), :],
                w_send.at[k], w_recv.at[k], dev,
            )
        col = pl.multiple_of(c * 256, 256)
        pltpu.make_async_copy(
            w_srcs[k].at[:, pl.ds(col, 256)],
            w.at[y, k, pl.ds(row, 16), :],
            w_recv.at[k],
        ).start()

    own = t_of(0, 0)

    def own_rows(n, dev, send, recv):
        for j, src in enumerate((in_ref, cot_ref)):
            remote(src, xc.at[own, c, j], send.at[n], recv, dev)

    w_first(0)
    own_rows(0, xr, a_send, a_recv.at[3, 0])
    own_rows(1, xleft, a_send, a_recv.at[1, 0])
    own_rows(2, zpart, a_send, a_recv.at[0, 1])
    w_first(1)
    w_first(2)
    own_rows(3, sib, a_send, s_recv.at[0, 0])
    for j, src in enumerate((in_ref, cot_ref)):
        pltpu.make_async_copy(src, xc.at[own, c, j], own_sem).start()

    def y_send_step(s, k):
        if s < 4:
            b = y_of((9 - s) % 8)
            remote(w.at[b, k], w.at[b, k], y_send.at[0, s - 1, k], y_recv.at[0, s - 1, k], yr)
            b = y_of(s - 1)
            remote(w.at[b, k], w.at[b, k], y_send.at[1, s - 1, k], y_recv.at[1, s - 1, k], yl)
        else:
            b = y_of(5)
            r = w.at[b, k, pl.ds(0, 64), :]
            remote(r, r, y_send.at[0, 3, k], y_recv.at[0, 3, k], yr)
            b = y_of(3)
            r = w.at[b, k, pl.ds(64, 64), :]
            remote(r, r, y_send.at[1, 3, k], y_recv.at[1, 3, k], yl)

    def y_wait_step(s, k):
        if s < 4:
            wait(w.at[y_of(8 - s), k], y_recv.at[0, s - 1, k])
            wait(w.at[y_of(s), k], y_recv.at[1, s - 1, k])
        else:
            b = y_of(4)
            wait(w.at[b, k, pl.ds(0, 64), :], y_recv.at[0, 3, k])
            wait(w.at[b, k, pl.ds(64, 64), :], y_recv.at[1, 3, k])

    def to_sibling(dx, dz):
        b = xc.at[t_of(dx, dz), c]
        remote(b, b, s_send.at[dx, dz], s_recv.at[dx, dz], sib)

    def a_wait(dx, dz):
        wait(xc.at[t_of(dx, dz), c], a_recv.at[dx, dz])

    def from_right(dz):
        a_wait(1, dz)
        b = xc.at[t_of(1, dz), c, 1]
        remote(b, b, a_send.at[6 + dz], a_recv.at[2, dz], xleft)
        to_sibling(1, dz)

    def from_left(dz):
        a_wait(3, dz)
        b = xc.at[t_of(3, dz), c, 0]
        remote(b, b, a_send.at[8 + dz], a_recv.at[2, dz], xr)
        to_sibling(3, dz)

    def s_wait(dx, dz):
        wait(xc.at[t_of(dx, dz), 1 - c], s_recv.at[dx, dz])

    def convert(tt, cc):
        rows = pl.ds(pl.multiple_of(cc * 256, 256), 256)
        v = xc[tt, cc, 0]
        hi, lo = split(v)
        xh[tt, rows, :] = hi
        xl[tt, rows, :] = lo
        hi, lo = split(jnp.transpose(v))
        xth[tt, :, rows] = hi
        xtl[tt, :, rows] = lo
        hi, lo = split(xc[tt, cc, 1])
        ch[tt, rows, :] = hi
        cl[tt, rows, :] = lo

    def convert_many(n, where):
        def body(i, carry):
            convert(*where(i))
            return carry

        lax.fori_loop(0, n, body, 0)

    for k in range(3):
        wait(w.at[y, k], w_recv.at[k])
        y_send_step(1, k)
        if k == 0:
            from_right(0)
            from_left(0)
    a_wait(0, 1)
    b = xc.at[t_of(0, 1), c]
    remote(b, b, a_send.at[4], a_recv.at[3, 1], xr)
    remote(b, b, a_send.at[5], a_recv.at[1, 1], xleft)
    to_sibling(0, 1)
    for k in range(3):
        y_wait_step(1, k)
        y_send_step(2, k)
    from_right(1)
    from_left(1)
    a_wait(2, 0)
    to_sibling(2, 0)
    pltpu.make_async_copy(xc.at[own, c], xc.at[own, c], own_sem).wait()
    s_wait(0, 0)
    s_wait(1, 0)
    s_wait(3, 0)
    convert_many(6, lambda i: (lax.rem(x + 3 + i // 2, NX) * NZL + zl, lax.rem(i, 2)))
    for k in range(3):
        y_wait_step(2, k)
        y_send_step(3, k)
    a_wait(2, 1)
    to_sibling(2, 1)
    for dx, dz in ((0, 1), (1, 1), (3, 1), (2, 0)):
        s_wait(dx, dz)
    convert_many(6, lambda i: (lax.rem(x + 3 + i // 2, NX) * NZL + 1 - zl, lax.rem(i, 2)))
    convert_many(2, lambda i: (lax.rem(x + 2, NX) * NZL + zl, i))
    s_wait(2, 1)
    convert_many(2, lambda i: (lax.rem(x + 2, NX) * NZL + 1 - zl, i))

    lhs = ((ch, cl), (xh, xl), (xh, xl))

    def forward(bs, k, first=False):
        n = 128 * len(bs)
        for i, b in enumerate(bs):
            hi, lo = split(w[b, k])
            wh[pl.ds(i * 128, 128), :] = hi
            wl[pl.ds(i * 128, 128), :] = lo
        ah, al = lhs[k]

        def body(r, carry):
            rows = pl.ds(pl.multiple_of(r * 256, 256), 256)
            if len(bs) == 2:
                h = jnp.concatenate([ah[b, rows, :] for b in bs], axis=1)
                l = jnp.concatenate([al[b, rows, :] for b in bs], axis=1)
            else:
                h = ah[bs[0], rows, :]
                l = al[bs[0], rows, :]
            v = dot3(h, l, wh[pl.ds(0, n), :], wl[pl.ds(0, n), :])
            if first:
                acc[k, rows, :] = v
            else:
                acc[k, rows, :] += v
            return carry

        lax.fori_loop(0, 2, body, 0)

    for k in range(3):
        forward((y,), k, True)
    for k in range(3):
        forward((y_of(1), y_of(7)), k)
    for k in range(3):
        y_wait_step(3, k)
        y_send_step(4, k)
    for k in range(3):
        forward((y_of(2), y_of(6)), k)
    for k in range(3):
        forward((y_of(3), y_of(5)), k)
    for k in range(3):
        y_wait_step(4, k)
        forward((y_of(4),), k)

    def rows_body(r, carry):
        rows = pl.ds(pl.multiple_of(r * 64, 64), 64)
        back = acc[0, rows, :]
        gate = acc[1, rows, :]
        lift = acc[2, rows, :]
        s = 1.0 / (1.0 + jnp.exp(-gate))
        bs = back * s
        hi, lo = split(bs * lift * (1.0 + gate * (1.0 - s)))
        rh[rows, 0:256] = hi
        rl[rows, 0:256] = lo
        hi, lo = split(bs * gate)
        rh[rows, 256:512] = hi
        rl[rows, 256:512] = lo
        return carry

    lax.fori_loop(0, 8, rows_body, 0)

    def backward(bs, m):
        if len(bs) == 2:
            h = jnp.concatenate([xth[b] for b in bs], axis=0)
            l = jnp.concatenate([xtl[b] for b in bs], axis=0)
        else:
            h, l = xth[bs[0]], xtl[bs[0]]
        cols = pl.ds(m * 256, 256)
        v = dot3(h, l, rh[:, cols], rl[:, cols])
        for i, b in enumerate(bs):
            gbuf[b, m] = v[i * 128 : (i + 1) * 128]

    def r_step(s, m):
        if s == 1:
            b = y_of(4)
            for d, dev in ((0, yr), (1, yl)):
                half = pl.ds(64 * d, 64)
                remote(
                    gbuf.at[b, m, half, :], rbuf.at[d, 0, m, half, :],
                    r_send.at[d, 0, m], r_recv.at[d, 0, m], dev,
                )
            return
        for d, dev in ((0, yr), (1, yl)):
            b = y_of(5 - s) if d == 0 else y_of(3 + s)
            if s == 2:
                half = pl.ds(64 * d, 64)
                wait(rbuf.at[d, 0, m, half, :], r_recv.at[d, 0, m])
                gbuf[b, m, half, :] += rbuf[d, 0, m, half, :]
            else:
                wait(rbuf.at[d, s - 2, m], r_recv.at[d, s - 2, m])
                gbuf[b, m] += rbuf[d, s - 2, m]
            remote(
                gbuf.at[b, m], rbuf.at[d, s - 1, m],
                r_send.at[d, s - 1, m], r_recv.at[d, s - 1, m], dev,
            )

    for m in range(2):
        backward((y_of(4),), m)
        r_step(1, m)
    for m in range(2):
        backward((y_of(3), y_of(5)), m)
    for m in range(2):
        r_step(2, m)
    for m in range(2):
        backward((y_of(2), y_of(6)), m)
    for m in range(2):
        r_step(3, m)
    for m in range(2):
        backward((y_of(1), y_of(7)), m)
    for m in range(2):
        r_step(4, m)
    for m in range(2):
        backward((y,), m)

    for m in range(2):
        wait(rbuf.at[0, 3, m], r_recv.at[0, 3, m])
        wait(rbuf.at[1, 3, m], r_recv.at[1, 3, m])
        for i in range(8):
            rows = pl.ds(16 * i, 16)
            tbuf[i, m] = gbuf[y, m, rows, :] + rbuf[0, 3, m, rows, :] + rbuf[1, 3, m, rows, :]
    src = zh * 2 + c
    for n, (dz, dc) in enumerate(zpeers):
        zz, cc, dev = zc_of(dz, dc)
        remote(tbuf.at[zz * 2 + cc], zbuf.at[src], z_send.at[n], z_recv, dev)
    zbuf[src] = tbuf[src]
    wait(zbuf.at[pl.ds(0, 7)], z_recv)
    for m in range(2):
        for cc in range(2):
            out_ref[m, :, cc * 256 : cc * 256 + 256] = (
                (zbuf[cc, m] + zbuf[2 + cc, m]) + (zbuf[4 + cc, m] + zbuf[6 + cc, m])
            )

    for k in range(3):
        wait(w.at[0, 0, pl.ds(0, 112), :], w_send.at[k])
    for n in range(6):
        wait(xc.at[0, 0], a_send.at[n])
    for n in range(6, 10):
        wait(xc.at[0, 0, 0], a_send.at[n])
    for dx in range(4):
        for dz in range(2):
            if (dx, dz) != (0, 0):
                wait(xc.at[0, 0], s_send.at[dx, dz])
    for d in range(2):
        for k in range(3):
            for s in range(4):
                n = 64 if s == 3 else 128
                wait(w.at[0, 0, pl.ds(0, n), :], y_send.at[d, s, k])
        for m in range(2):
            for s in range(4):
                n = 64 if s == 0 else 128
                wait(gbuf.at[0, 0, pl.ds(0, n), :], r_send.at[d, s, m])
    for n in range(7):
        wait(tbuf.at[0], z_send.at[n])


def grads(inputs, cotangent, gate_weight, up_weight, down_weight):
    dma = pltpu.SemaphoreType.DMA
    return pl.pallas_call(
        kernel,
        name="grads",
        out_shape=jax.ShapeDtypeStruct((2, 16, 512), F32),
        in_specs=[pl.BlockSpec(memory_space=pl.ANY)] * 5,
        out_specs=pl.BlockSpec(memory_space=pltpu.VMEM),
        scratch_shapes=[
            pltpu.VMEM((8, 2, 2, 256, 128), F32),
            pltpu.VMEM((8, 3, 128, 256), F32),
            pltpu.VMEM((8, 512, 128), BF16),
            pltpu.VMEM((8, 512, 128), BF16),
            pltpu.VMEM((8, 512, 128), BF16),
            pltpu.VMEM((8, 512, 128), BF16),
            pltpu.VMEM((8, 128, 512), BF16),
            pltpu.VMEM((8, 128, 512), BF16),
            pltpu.VMEM((256, 256), BF16),
            pltpu.VMEM((256, 256), BF16),
            pltpu.VMEM((3, 512, 256), F32),
            pltpu.VMEM((512, 512), BF16),
            pltpu.VMEM((512, 512), BF16),
            pltpu.VMEM((8, 2, 128, 256), F32),
            pltpu.VMEM((2, 4, 2, 128, 256), F32),
            pltpu.VMEM((8, 2, 16, 256), F32),
            pltpu.VMEM((8, 2, 16, 256), F32),
            dma,
            dma((4, 2)),
            dma((10,)),
            dma((4, 2)),
            dma((4, 2)),
            dma((3,)),
            dma((3,)),
            dma((2, 4, 3)),
            dma((2, 4, 3)),
            dma((2, 4, 2)),
            dma((2, 4, 2)),
            dma,
            dma((7,)),
        ],
        compiler_params=pltpu.CompilerParams(
            collective_id=0, has_side_effects=True, vmem_limit_bytes=48 * 1024 * 1024
        ),
    )(inputs, cotangent, gate_weight, up_weight, down_weight)


def local(
    inputs,
    cotangent,
    gate_weight,
    up_weight,
    down_weight,
    gate_first,
    gate_second,
    up_first,
    up_second,
):
    g = grads(inputs, cotangent, gate_weight, up_weight, down_weight)
    gate_new, gate_first_new, gate_second_new = adam_update(
        gate_weight, gate_first, gate_second, g[0]
    )
    up_new, up_first_new, up_second_new = adam_update(up_weight, up_first, up_second, g[1])
    return (gate_new, gate_first_new, gate_second_new, up_new, up_first_new, up_second_new)


def solution(mesh):
    spec = P("dp", "tensor")
    return jax.shard_map(
        local, mesh=mesh, in_specs=(spec,) * 9, out_specs=(spec,) * 6, check_vma=False
    )
```

```python
import jax
import jax.numpy as jnp
from jax import lax
from jax.experimental import pallas as pl
from jax.experimental.pallas import tpu as pltpu
from jax.sharding import PartitionSpec as P

STEP = 100
MESH = pl.DeviceIdType.MESH
F32 = jnp.float32
BF16 = jnp.bfloat16
NX, NZL, NY, NZH = 4, 2, 8, 4


def adam_update(weight, first, second, grad):
    first_new = 0.9 * first + 0.1 * grad
    second_new = 0.95 * second + 0.05 * grad * grad
    first_hat = first_new / (1.0 - 0.9**STEP)
    second_hat = second_new / (1.0 - 0.95**STEP)
    weight_new = weight - 0.003 * first_hat / (jnp.sqrt(second_hat) + 1e-08)
    return (weight_new, first_new, second_new)


def split(v):
    hi = v.astype(BF16)
    return hi, (v - hi.astype(F32)).astype(BF16)


def dot(a, b):
    return jnp.dot(a, b, preferred_element_type=F32)


def dot3(ah, al, bh, bl):
    return dot(ah, bh) + dot(ah, bl) + dot(al, bh)


def kernel(
    in_ref, cot_ref, gw_ref, uw_ref, dw_ref, out_ref,
    xc, w, xh, xl, ch, cl, xth, xtl, wh, wl, acc, rh, rl, gbuf, rbuf, tbuf, zbuf,
    own_sem, a_recv, a_send, s_recv, s_send, w_recv, w_send, y_recv, y_send,
    u_recv, u_send, uy_recv, uy_send, uz_recv, uz_send, r_recv, r_send, z_recv, z_send,
):
    dp = lax.axis_index("dp")
    t = lax.axis_index("tensor")
    c = lax.rem(dp, 2)
    zh = lax.rem(dp // 2, NZH)
    y = dp // (2 * NZH)
    x = t // NZL
    zl = lax.rem(t, NZL)

    def t_of(dx, dz):
        zz = zl if dz == 0 else 1 - zl
        return lax.rem(x + dx, NX) * NZL + zz

    def y_of(d):
        return lax.rem(y + d, NY)

    def dp_of(yy, zz, cc):
        return (yy * NZH + zz) * 2 + cc

    sib = (dp_of(y, zh, 1 - c), t)
    zpart = (dp, t_of(0, 1))
    xr = (dp, t_of(1, 0))
    xleft = (dp, t_of(3, 0))
    yr = (dp_of(y_of(1), zh, c), t)
    yl = (dp_of(y_of(7), zh, c), t)

    def zc_of(dz, dc):
        zz = lax.rem(zh + dz, NZH)
        cc = c if dc == 0 else 1 - c
        return zz, cc, (dp_of(y, zz, cc), t)

    zpeers = [(dz, dc) for dz in range(NZH) for dc in range(2) if (dz, dc) != (0, 0)]

    barrier = pltpu.get_barrier_semaphore()
    peers = [zc_of(dz, dc)[2] for dz, dc in zpeers] + [zpart, xr, xleft, yr, yl]
    for peer in peers:
        pl.semaphore_signal(barrier, inc=1, device_id=peer, device_id_type=MESH)
    pl.semaphore_wait(barrier, len(peers))

    def remote(src, dst, send, recv, dev):
        pltpu.make_async_remote_copy(
            src_ref=src, dst_ref=dst, send_sem=send, recv_sem=recv,
            device_id=dev, device_id_type=MESH,
        ).start()

    def wait(ref, sem):
        pltpu.make_async_copy(ref, ref, sem).wait()

    w_srcs = (dw_ref, gw_ref)

    def w_first(k):
        row = pl.multiple_of(zh * 32 + c * 16, 16)
        for dz, dc in [(1, 0), (1, 1), (3, 0), (3, 1), (2, 0), (2, 1), (0, 1)]:
            _, cc, dev = zc_of(dz, dc)
            col = pl.multiple_of(cc * 256, 256)
            remote(
                w_srcs[k].at[:, pl.ds(col, 256)],
                w.at[y, k, pl.ds(row, 16), :],
                w_send.at[k], w_recv.at[k], dev,
            )
        col = pl.multiple_of(c * 256, 256)
        pltpu.make_async_copy(
            w_srcs[k].at[:, pl.ds(col, 256)],
            w.at[y, k, pl.ds(row, 16), :],
            w_recv.at[k],
        ).start()

    own = t_of(0, 0)

    def own_rows(n, dev, send, recv):
        for j, src in enumerate((in_ref, cot_ref)):
            remote(src, xc.at[own, c, j], send.at[n], recv, dev)

    def zrows(zz, first=0, n=32):
        return pl.ds(pl.multiple_of(zz * 32 + first, 16), n)

    zr, zleft = zc_of(1, 0)[2], zc_of(3, 0)[2]
    zat = [lax.rem(zh + d, NZH) for d in range(NZH)]

    def u_first():
        mine = zrows(zh, c * 16, 16)
        col = pl.multiple_of((1 - c) * 256, 256)
        remote(uw_ref.at[:, pl.ds(col, 256)], w.at[y, 2, mine, :], u_send, u_recv, sib)
        col = pl.multiple_of(c * 256, 256)
        pltpu.make_async_copy(uw_ref.at[:, pl.ds(col, 256)], w.at[y, 2, mine, :], u_recv).start()

    def u_parts(s, back):
        if s < 4:
            lo, hi = y_of((9 - s - back) % 8), y_of(s - 1 + back)
            return (w.at[lo, 2, zrows(zh), :], w.at[hi, 2, zrows(zh), :])
        lo, hi = y_of(5 - back), y_of(3 + back)
        return (w.at[lo, 2, zrows(zh, 0, 16), :], w.at[hi, 2, zrows(zh, 16, 16), :])

    def u_y_send(s):
        for d, r in enumerate(u_parts(s, 0)):
            remote(r, r, uy_send.at[d, s - 1], uy_recv.at[d, s - 1], (yr, yl)[d])

    def u_y_wait(s):
        for d, r in enumerate(u_parts(s, 1)):
            wait(r, uy_recv.at[d, s - 1])

    def u_group(g, zz, first=0, n=32):
        return w.at[pl.ds(2 * g, 2), 2, zrows(zz, first, n), :]

    def u_z_send(g):
        r = u_group(g, zh)
        for d in range(2):
            remote(r, r, uz_send.at[0, d, g], uz_recv.at[0, d, g], (zr, zleft)[d])

    def u_z_relay(g):
        for d, zz in enumerate((zat[3], zat[1])):
            wait(u_group(g, zz), uz_recv.at[0, d, g])
            r = u_group(g, zz, 16 * d, 16)
            remote(r, r, uz_send.at[1, d, g], uz_recv.at[1, d, g], (zr, zleft)[d])

    def u_z_end(g):
        for d in range(2):
            wait(u_group(g, zat[2], 16 * d, 16), uz_recv.at[1, d, g])

    w_first(0)
    own_rows(0, xr, a_send, a_recv.at[3, 0])
    own_rows(1, xleft, a_send, a_recv.at[1, 0])
    u_first()
    w_first(1)
    own_rows(2, zpart, a_send, a_recv.at[0, 1])
    own_rows(3, sib, a_send, s_recv.at[0, 0])
    for j, src in enumerate((in_ref, cot_ref)):
        pltpu.make_async_copy(src, xc.at[own, c, j], own_sem).start()

    def y_send_step(s, k):
        if s < 4:
            b = y_of((9 - s) % 8)
            remote(w.at[b, k], w.at[b, k], y_send.at[0, s - 1, k], y_recv.at[0, s - 1, k], yr)
            b = y_of(s - 1)
            remote(w.at[b, k], w.at[b, k], y_send.at[1, s - 1, k], y_recv.at[1, s - 1, k], yl)
        else:
            b = y_of(5)
            r = w.at[b, k, pl.ds(0, 64), :]
            remote(r, r, y_send.at[0, 3, k], y_recv.at[0, 3, k], yr)
            b = y_of(3)
            r = w.at[b, k, pl.ds(64, 64), :]
            remote(r, r, y_send.at[1, 3, k], y_recv.at[1, 3, k], yl)

    def y_wait_step(s, k):
        if s < 4:
            wait(w.at[y_of(8 - s), k], y_recv.at[0, s - 1, k])
            wait(w.at[y_of(s), k], y_recv.at[1, s - 1, k])
        else:
            b = y_of(4)
            wait(w.at[b, k, pl.ds(0, 64), :], y_recv.at[0, 3, k])
            wait(w.at[b, k, pl.ds(64, 64), :], y_recv.at[1, 3, k])

    def to_sibling(dx, dz):
        b = xc.at[t_of(dx, dz), c]
        remote(b, b, s_send.at[dx, dz], s_recv.at[dx, dz], sib)

    def a_wait(dx, dz):
        wait(xc.at[t_of(dx, dz), c], a_recv.at[dx, dz])

    def from_right(dz):
        a_wait(1, dz)
        b = xc.at[t_of(1, dz), c, 1]
        remote(b, b, a_send.at[6 + dz], a_recv.at[2, dz], xleft)
        to_sibling(1, dz)

    def from_left(dz):
        a_wait(3, dz)
        b = xc.at[t_of(3, dz), c, 0]
        remote(b, b, a_send.at[8 + dz], a_recv.at[2, dz], xr)
        to_sibling(3, dz)

    def s_wait(dx, dz):
        wait(xc.at[t_of(dx, dz), 1 - c], s_recv.at[dx, dz])

    def convert(tt, cc):
        rows = pl.ds(pl.multiple_of(cc * 256, 256), 256)
        v = xc[tt, cc, 0]
        hi, lo = split(v)
        xh[tt, rows, :] = hi
        xl[tt, rows, :] = lo
        hi, lo = split(jnp.transpose(v))
        xth[tt, :, rows] = hi
        xtl[tt, :, rows] = lo
        hi, lo = split(xc[tt, cc, 1])
        ch[tt, rows, :] = hi
        cl[tt, rows, :] = lo

    def convert_many(n, where):
        def body(i, carry):
            convert(*where(i))
            return carry

        lax.fori_loop(0, n, body, 0)

    def y_next(s, k):
        y_wait_step(s, k)
        y_send_step(s + 1, k)

    wait(w.at[y, 2, zrows(zh), :], u_recv)
    u_y_send(1)
    for s in range(1, 3):
        u_y_wait(s)
        u_y_send(s + 1)
    wait(w.at[y, 0], w_recv.at[0])
    y_send_step(1, 0)
    from_right(0)
    from_left(0)
    u_y_wait(3)
    u_y_send(4)
    wait(w.at[y, 1], w_recv.at[1])
    y_send_step(1, 1)
    u_y_wait(4)
    for g in range(4):
        u_z_send(g)
    y_next(1, 0)
    a_wait(0, 1)
    b = xc.at[t_of(0, 1), c]
    remote(b, b, a_send.at[4], a_recv.at[3, 1], xr)
    remote(b, b, a_send.at[5], a_recv.at[1, 1], xleft)
    to_sibling(0, 1)
    a_wait(2, 0)
    to_sibling(2, 0)
    y_next(1, 1)
    pltpu.make_async_copy(xc.at[own, c], xc.at[own, c], own_sem).wait()
    s_wait(0, 0)
    s_wait(1, 0)
    s_wait(3, 0)
    convert_many(6, lambda i: (lax.rem(x + 3 + i // 2, NX) * NZL + zl, lax.rem(i, 2)))
    u_z_relay(0)
    y_next(2, 0)
    s_wait(0, 1)
    s_wait(2, 0)
    convert_many(2, lambda i: (x * NZL + 1 - zl, i))
    convert_many(2, lambda i: (lax.rem(x + 2, NX) * NZL + zl, i))
    y_next(2, 1)
    from_right(1)
    from_left(1)
    u_z_relay(1)
    y_next(3, 0)
    s_wait(1, 1)
    s_wait(3, 1)
    convert_many(4, lambda i: (lax.rem(x + 3 + 2 * (i // 2), NX) * NZL + 1 - zl, lax.rem(i, 2)))
    u_z_relay(2)
    a_wait(2, 1)
    to_sibling(2, 1)
    y_next(3, 1)
    s_wait(2, 1)
    convert_many(2, lambda i: (lax.rem(x + 2, NX) * NZL + 1 - zl, i))

    lhs = ((ch, cl), (xh, xl), (xh, xl))

    def forward(bs, k, first=False):
        n = 128 * len(bs)
        for i, b in enumerate(bs):
            hi, lo = split(w[b, k])
            wh[pl.ds(i * 128, 128), :] = hi
            wl[pl.ds(i * 128, 128), :] = lo
        ah, al = lhs[k]

        def body(r, carry):
            rows = pl.ds(pl.multiple_of(r * 256, 256), 256)
            if len(bs) == 2:
                h = jnp.concatenate([ah[b, rows, :] for b in bs], axis=1)
                l = jnp.concatenate([al[b, rows, :] for b in bs], axis=1)
            else:
                h = ah[bs[0], rows, :]
                l = al[bs[0], rows, :]
            v = dot3(h, l, wh[pl.ds(0, n), :], wl[pl.ds(0, n), :])
            if first:
                acc[k, rows, :] = v
            else:
                acc[k, rows, :] += v
            return carry

        lax.fori_loop(0, 2, body, 0)

    for k in range(2):
        forward((y,), k, True)
    u_z_relay(3)
    for d in range(1, 4):
        for k in range(2):
            forward((y_of(d), y_of(8 - d)), k)
    for k in range(2):
        y_wait_step(4, k)
        forward((y_of(4),), k)
    for g in range(4):
        u_z_end(g)
        forward((2 * g, 2 * g + 1), 2, g == 0)

    def rows_body(r, carry):
        rows = pl.ds(pl.multiple_of(r * 64, 64), 64)
        back = acc[0, rows, :]
        gate = acc[1, rows, :]
        lift = acc[2, rows, :]
        s = 1.0 / (1.0 + jnp.exp(-gate))
        bs = back * s
        hi, lo = split(bs * lift * (1.0 + gate * (1.0 - s)))
        rh[rows, 0:256] = hi
        rl[rows, 0:256] = lo
        hi, lo = split(bs * gate)
        rh[rows, 256:512] = hi
        rl[rows, 256:512] = lo
        return carry

    lax.fori_loop(0, 8, rows_body, 0)

    def backward(bs, m):
        if len(bs) == 2:
            h = jnp.concatenate([xth[b] for b in bs], axis=0)
            l = jnp.concatenate([xtl[b] for b in bs], axis=0)
        else:
            h, l = xth[bs[0]], xtl[bs[0]]
        cols = pl.ds(m * 256, 256)
        v = dot3(h, l, rh[:, cols], rl[:, cols])
        for i, b in enumerate(bs):
            gbuf[b, m] = v[i * 128 : (i + 1) * 128]

    def r_step(s, m):
        if s == 1:
            b = y_of(4)
            for d, dev in ((0, yr), (1, yl)):
                half = pl.ds(64 * d, 64)
                remote(
                    gbuf.at[b, m, half, :], rbuf.at[d, 0, m, half, :],
                    r_send.at[d, 0, m], r_recv.at[d, 0, m], dev,
                )
            return
        for d, dev in ((0, yr), (1, yl)):
            b = y_of(5 - s) if d == 0 else y_of(3 + s)
            if s == 2:
                half = pl.ds(64 * d, 64)
                wait(rbuf.at[d, 0, m, half, :], r_recv.at[d, 0, m])
                gbuf[b, m, half, :] += rbuf[d, 0, m, half, :]
            else:
                wait(rbuf.at[d, s - 2, m], r_recv.at[d, s - 2, m])
                gbuf[b, m] += rbuf[d, s - 2, m]
            remote(
                gbuf.at[b, m], rbuf.at[d, s - 1, m],
                r_send.at[d, s - 1, m], r_recv.at[d, s - 1, m], dev,
            )

    for m in range(2):
        backward((y_of(4),), m)
        r_step(1, m)
    for m in range(2):
        backward((y_of(3), y_of(5)), m)
    for m in range(2):
        r_step(2, m)
    for m in range(2):
        backward((y_of(2), y_of(6)), m)
    for m in range(2):
        r_step(3, m)
    for m in range(2):
        backward((y_of(1), y_of(7)), m)
    for m in range(2):
        r_step(4, m)
    for m in range(2):
        backward((y,), m)

    src = zh * 2 + c
    for m in range(2):
        wait(rbuf.at[0, 3, m], r_recv.at[0, 3, m])
        wait(rbuf.at[1, 3, m], r_recv.at[1, 3, m])
        for i in range(8):
            rows = pl.ds(16 * i, 16)
            tbuf[m, i] = gbuf[y, m, rows, :] + rbuf[0, 3, m, rows, :] + rbuf[1, 3, m, rows, :]
        for n, (dz, dc) in enumerate(zpeers):
            zz, cc, dev = zc_of(dz, dc)
            remote(tbuf.at[m, zz * 2 + cc], zbuf.at[m, src], z_send.at[m, n], z_recv.at[m], dev)
        zbuf[m, src] = tbuf[m, src]
    for m in range(2):
        wait(zbuf.at[m, pl.ds(0, 7)], z_recv.at[m])
        for cc in range(2):
            out_ref[m, :, cc * 256 : cc * 256 + 256] = (
                (zbuf[m, cc] + zbuf[m, 2 + cc]) + (zbuf[m, 4 + cc] + zbuf[m, 6 + cc])
            )

    for k in range(2):
        wait(w.at[0, 0, pl.ds(0, 112), :], w_send.at[k])
    wait(w.at[0, 0, pl.ds(0, 16), :], u_send)
    for n in range(6):
        wait(xc.at[0, 0], a_send.at[n])
    for n in range(6, 10):
        wait(xc.at[0, 0, 0], a_send.at[n])
    for dx in range(4):
        for dz in range(2):
            if (dx, dz) != (0, 0):
                wait(xc.at[0, 0], s_send.at[dx, dz])
    for d in range(2):
        for k in range(2):
            for s in range(4):
                n = 64 if s == 3 else 128
                wait(w.at[0, 0, pl.ds(0, n), :], y_send.at[d, s, k])
        for s in range(4):
            n = 16 if s == 3 else 32
            wait(w.at[0, 0, pl.ds(0, n), :], uy_send.at[d, s])
        for g in range(4):
            wait(w.at[0, 0, pl.ds(0, 64), :], uz_send.at[0, d, g])
            wait(w.at[0, 0, pl.ds(0, 32), :], uz_send.at[1, d, g])
        for m in range(2):
            for s in range(4):
                n = 64 if s == 0 else 128
                wait(gbuf.at[0, 0, pl.ds(0, n), :], r_send.at[d, s, m])
    for m in range(2):
        for n in range(7):
            wait(tbuf.at[0, 0], z_send.at[m, n])


def grads(inputs, cotangent, gate_weight, up_weight, down_weight):
    dma = pltpu.SemaphoreType.DMA
    return pl.pallas_call(
        kernel,
        name="grads",
        out_shape=jax.ShapeDtypeStruct((2, 16, 512), F32),
        in_specs=[pl.BlockSpec(memory_space=pl.ANY)] * 5,
        out_specs=pl.BlockSpec(memory_space=pltpu.VMEM),
        scratch_shapes=[
            pltpu.VMEM((8, 2, 2, 256, 128), F32),
            pltpu.VMEM((8, 3, 128, 256), F32),
            pltpu.VMEM((8, 512, 128), BF16),
            pltpu.VMEM((8, 512, 128), BF16),
            pltpu.VMEM((8, 512, 128), BF16),
            pltpu.VMEM((8, 512, 128), BF16),
            pltpu.VMEM((8, 128, 512), BF16),
            pltpu.VMEM((8, 128, 512), BF16),
            pltpu.VMEM((256, 256), BF16),
            pltpu.VMEM((256, 256), BF16),
            pltpu.VMEM((3, 512, 256), F32),
            pltpu.VMEM((512, 512), BF16),
            pltpu.VMEM((512, 512), BF16),
            pltpu.VMEM((8, 2, 128, 256), F32),
            pltpu.VMEM((2, 4, 2, 128, 256), F32),
            pltpu.VMEM((2, 8, 16, 256), F32),
            pltpu.VMEM((2, 8, 16, 256), F32),
            dma,
            dma((4, 2)),
            dma((10,)),
            dma((4, 2)),
            dma((4, 2)),
            dma((2,)),
            dma((2,)),
            dma((2, 4, 2)),
            dma((2, 4, 2)),
            dma,
            dma,
            dma((2, 4)),
            dma((2, 4)),
            dma((2, 2, 4)),
            dma((2, 2, 4)),
            dma((2, 4, 2)),
            dma((2, 4, 2)),
            dma((2,)),
            dma((2, 7)),
        ],
        compiler_params=pltpu.CompilerParams(
            collective_id=0, has_side_effects=True, vmem_limit_bytes=67043328
        ),
    )(inputs, cotangent, gate_weight, up_weight, down_weight)


def local(
    inputs,
    cotangent,
    gate_weight,
    up_weight,
    down_weight,
    gate_first,
    gate_second,
    up_first,
    up_second,
):
    g = grads(inputs, cotangent, gate_weight, up_weight, down_weight)
    gate_new, gate_first_new, gate_second_new = adam_update(
        gate_weight, gate_first, gate_second, g[0]
    )
    up_new, up_first_new, up_second_new = adam_update(up_weight, up_first, up_second, g[1])
    return (gate_new, gate_first_new, gate_second_new, up_new, up_first_new, up_second_new)


def solution(mesh):
    spec = P("dp", "tensor")
    return jax.shard_map(
        local, mesh=mesh, in_specs=(spec,) * 9, out_specs=(spec,) * 6, check_vma=False
    )
```

```python
import jax
import jax.numpy as jnp
from jax import lax
from jax.experimental import pallas as pl
from jax.experimental.pallas import tpu as pltpu
from jax.sharding import PartitionSpec as P

STEP = 100
MESH = pl.DeviceIdType.MESH
F32 = jnp.float32
BF16 = jnp.bfloat16
NX, NZL, NY, NZH = 4, 2, 8, 4


def adam_update(weight, first, second, grad):
    first_new = 0.9 * first + 0.1 * grad
    second_new = 0.95 * second + 0.05 * grad * grad
    first_hat = first_new / (1.0 - 0.9**STEP)
    second_hat = second_new / (1.0 - 0.95**STEP)
    weight_new = weight - 0.003 * first_hat / (jnp.sqrt(second_hat) + 1e-08)
    return (weight_new, first_new, second_new)


def split(v):
    hi = v.astype(BF16)
    return hi, (v - hi.astype(F32)).astype(BF16)


def dot(a, b):
    return jnp.dot(a, b, preferred_element_type=F32)


def dot3(ah, al, bh, bl):
    return dot(ah, bh) + dot(ah, bl) + dot(al, bh)


def kernel(
    in_ref, cot_ref, gw_ref, uw_ref, dw_ref, out_ref,
    xc, w, xh, xl, ch, cl, xth, xtl, acc, rh, rl,
    gbuf, rbuf, tbuf, zbuf, gz, rz1, rz2, yz,
    own_sem, a_recv, a_send, s_recv, s_send, o_recv, o_send, w_recv, w_send, y_recv, y_send,
    u_recv, u_send, r_recv, r_send, z_recv, z_send, f_recv, f_send, g_recv, g_send,
):
    dp = lax.axis_index("dp")
    t = lax.axis_index("tensor")
    c = lax.rem(dp, 2)
    zh = lax.rem(dp // 2, NZH)
    y = dp // (2 * NZH)
    x = t // NZL
    zl = lax.rem(t, NZL)

    def t_of(dx, dz):
        zz = zl if dz == 0 else 1 - zl
        return lax.rem(x + dx, NX) * NZL + zz

    def y_of(d):
        return lax.rem(y + d, NY)

    def core_of(dc):
        return c if dc == 0 else 1 - c

    def dev_of(dy, dz, dc):
        return ((y_of(dy) * NZH + zat[dz]) * 2 + core_of(dc), t)

    zat = [lax.rem(zh + d, NZH) for d in range(NZH)]
    sib = dev_of(0, 0, 1)
    zpart = (dp, t_of(0, 1))
    xs = ((dp, t_of(1, 0)), (dp, t_of(3, 0)))
    ys = (dev_of(1, 0, 0), dev_of(7, 0, 0))
    zs = (dev_of(0, 1, 0), dev_of(0, 3, 0))
    zpeers = [(2, 0), (2, 1), (1, 0), (3, 0), (1, 1), (3, 1)]
    ypeers = [(dy, dc) for dy in (4, 3, 5, 2, 6, 1, 7) for dc in range(2)]

    barrier = pltpu.get_barrier_semaphore()
    peers = [dev_of(0, dz, dc) for dz, dc in zpeers] + [sib, zpart, xs[0], xs[1]]
    peers = peers + [dev_of(dy, 0, dc) for dy, dc in ypeers]
    for peer in peers:
        pl.semaphore_signal(barrier, inc=1, device_id=peer, device_id_type=MESH)
    pl.semaphore_wait(barrier, len(peers))

    def remote(src, dst, send, recv, dev):
        pltpu.make_async_remote_copy(
            src_ref=src, dst_ref=dst, send_sem=send, recv_sem=recv,
            device_id=dev, device_id_type=MESH,
        ).start()

    def local_copy(src, dst, sem):
        pltpu.make_async_copy(src, dst, sem).start()

    def wait(ref, sem):
        pltpu.make_async_copy(ref, ref, sem).wait()

    w_srcs = (dw_ref, gw_ref, uw_ref)

    def w_own(k):
        mine = pl.ds(pl.multiple_of(c * 16, 16), 16)
        n = k // 2
        there = pl.ds(pl.multiple_of((1 - c) * 256, 256), 256)
        remote(w_srcs[k].at[:, there], w.at[y, k, mine, :], o_send.at[n], o_recv.at[n], sib)
        here = pl.ds(pl.multiple_of(c * 256, 256), 256)
        local_copy(w_srcs[k].at[:, here], w.at[y, k, mine, :], o_recv.at[n])

    def w_first(k):
        for dz, dc in zpeers:
            src = w_srcs[k].at[:, pl.ds(pl.multiple_of(core_of(dc) * 256, 256), 256)]
            rows = pl.ds(pl.multiple_of((4 - dz) * 32 + c * 16, 16), 16)
            remote(src, w.at[y, k, rows, :], w_send.at[k], w_recv.at[k], dev_of(0, dz, dc))

    U, A, B0, B1 = range(4)

    def part(ring, b, half):
        if ring == A:
            return w.at[b, pl.ds(0, 2), pl.ds(0, 32), :] if half is None else w.at[b, half, pl.ds(0, 32), :]
        k = (2, 0, 0, 1)[ring]
        first, n = (0, 32) if ring == U else (32, 96)
        if half is not None:
            n = n // 2
            first = first + half * n
        return w.at[b, k, pl.ds(first, n), :]

    def step_parts(ring, s, back):
        if s < 4:
            return part(ring, y_of((9 - s - back) % 8), None), part(ring, y_of(s - 1 + back), None)
        return part(ring, y_of(5 - back), 0), part(ring, y_of(3 + back), 1)

    def y_start(ring, s):
        for d, r in enumerate(step_parts(ring, s, 0)):
            remote(r, r, y_send.at[d, s - 1, ring], y_recv.at[d, s - 1, ring], ys[d])

    def y_end(ring, s):
        for d, r in enumerate(step_parts(ring, s, 1)):
            wait(r, y_recv.at[d, s - 1, ring])

    def y_next(ring, s):
        y_end(ring, s)
        y_start(ring, s + 1)

    def u_start(i):
        b = y_of(i)
        for d, first in enumerate((96, 32)):
            remote(
                w.at[b, 2, pl.ds(0, 32), :], w.at[b, 2, pl.ds(first, 32), :],
                u_send.at[0, d, i], u_recv.at[0, d, i], zs[d],
            )

    def u_relay(i):
        b = y_of(i)
        for d, (first, src, dst) in enumerate(((96, 96, 64), (32, 48, 80))):
            wait(w.at[b, 2, pl.ds(first, 32), :], u_recv.at[0, d, i])
            remote(
                w.at[b, 2, pl.ds(src, 16), :], w.at[b, 2, pl.ds(dst, 16), :],
                u_send.at[1, d, i], u_recv.at[1, d, i], zs[d],
            )

    def u_end(i):
        for d in range(2):
            wait(w.at[y_of(i), 2, pl.ds(64 + 16 * d, 16), :], u_recv.at[1, d, i])

    own = t_of(0, 0)
    rows_src = (in_ref, cot_ref)

    def own_to(n, j, dev, recv):
        remote(rows_src[j], xc.at[own, c, j], a_send.at[n + j], recv, dev)

    def pass_on(n, dx, dz, j, d, to_dx):
        b = xc.at[t_of(dx, dz), c, j]
        remote(b, b, a_send.at[n], a_recv.at[to_dx, dz, j], xs[d])

    def a_end(dx, dz, j):
        wait(xc.at[t_of(dx, dz), c, j], a_recv.at[dx, dz, j])

    def from_right(dz):
        a_end(1, dz, 1)
        pass_on(10 + dz, 1, dz, 1, 1, 2)

    def from_left(dz):
        a_end(3, dz, 0)
        pass_on(12 + dz, 3, dz, 0, 0, 2)

    def to_sibling(dx, dz):
        b = xc.at[t_of(dx, dz), c]
        remote(b, b, s_send.at[dx, dz], s_recv.at[dx, dz], sib)

    def s_end(dx, dz):
        wait(xc.at[t_of(dx, dz), 1 - c], s_recv.at[dx, dz])

    def convert(tt, cc):
        rows = pl.ds(pl.multiple_of(cc * 256, 256), 256)
        v = xc[tt, cc, 0]
        hi, lo = split(v)
        xh[tt, rows, :] = hi
        xl[tt, rows, :] = lo
        hi, lo = split(jnp.transpose(v))
        xth[tt, :, rows] = hi
        xtl[tt, :, rows] = lo
        hi, lo = split(xc[tt, cc, 1])
        ch[tt, rows, :] = hi
        cl[tt, rows, :] = lo

    def convert_many(n, where):
        def body(i, carry):
            convert(*where(i))
            return carry

        lax.fori_loop(0, n, body, 0)

    lhs = ((ch, cl), (xh, xl), (xh, xl))
    w_rows = [pl.ds(pl.multiple_of(lax.rem(j + NZH - zh, NZH) * 32, 32), 32) for j in range(NZH)]

    def forward(bs, k, first=False):
        wh, wl = split(jnp.concatenate([w[b, k, r, :] for b in bs for r in w_rows], axis=0))
        ah, al = lhs[k]
        if len(bs) == 2:
            h = jnp.concatenate([ah[b] for b in bs], axis=1)
            l = jnp.concatenate([al[b] for b in bs], axis=1)
        else:
            h, l = ah[bs[0]], al[bs[0]]
        v = dot3(h, l, wh, wl)
        if first:
            acc[k] = v
        else:
            acc[k] += v

    w_own(2)
    w_own(0)
    w_own(1)
    for j in range(2):
        own_to(0, j, xs[0], a_recv.at[3, 0, j])
        own_to(2, j, xs[1], a_recv.at[1, 0, j])
    w_first(0)
    w_first(1)
    for j in range(2):
        own_to(4, j, zpart, a_recv.at[0, 1, j])
    for j in range(2):
        remote(rows_src[j], xc.at[own, c, j], s_send.at[0, 0], s_recv.at[0, 0], sib)
        local_copy(rows_src[j], xc.at[own, c, j], own_sem)

    wait(part(U, y, None), o_recv.at[1])
    y_start(U, 1)
    u_start(0)
    wait(part(A, y, None), o_recv.at[0])
    y_start(A, 1)
    y_next(U, 1)
    u_start(1)
    u_start(7)
    y_next(A, 1)
    y_next(U, 2)
    u_start(2)
    u_start(6)
    from_left(0)
    wait(part(B0, y, None), w_recv.at[0])
    y_start(B0, 1)
    from_right(0)
    a_end(1, 0, 0)
    to_sibling(1, 0)
    a_end(3, 0, 1)
    to_sibling(3, 0)
    y_next(A, 2)
    y_next(U, 3)
    u_start(3)
    u_start(5)
    wait(part(B1, y, None), w_recv.at[1])
    y_start(B1, 1)
    a_end(0, 1, 0)
    pass_on(6, 0, 1, 0, 0, 3)
    pass_on(8, 0, 1, 0, 1, 1)
    y_next(B0, 1)
    for j in range(2):
        a_end(2, 0, j)
    to_sibling(2, 0)
    y_next(A, 3)
    y_end(U, 4)
    u_start(4)
    a_end(0, 1, 1)
    pass_on(9, 0, 1, 1, 1, 1)
    pass_on(7, 0, 1, 1, 0, 3)
    to_sibling(0, 1)
    wait(xc.at[own, c], own_sem)
    s_end(0, 0)
    s_end(1, 0)
    s_end(3, 0)
    convert_many(6, lambda i: (lax.rem(x + 3 + i // 2, NX) * NZL + zl, lax.rem(i, 2)))
    from_left(1)
    y_next(B1, 1)
    u_relay(0)
    y_next(B0, 2)
    s_end(2, 0)
    convert_many(2, lambda i: (lax.rem(x + 2, NX) * NZL + zl, i))
    s_end(0, 1)
    convert_many(2, lambda i: (x * NZL + 1 - zl, i))
    from_right(1)
    a_end(1, 1, 0)
    to_sibling(1, 1)
    a_end(3, 1, 1)
    to_sibling(3, 1)
    u_relay(1)
    u_relay(7)
    y_next(B1, 2)
    u_relay(2)
    u_relay(6)
    y_next(B0, 3)
    s_end(1, 1)
    s_end(3, 1)
    convert_many(4, lambda i: (lax.rem(x + 3 + 2 * (i // 2), NX) * NZL + 1 - zl, lax.rem(i, 2)))
    for j in range(2):
        a_end(2, 1, j)
    to_sibling(2, 1)
    u_relay(3)
    u_relay(5)
    y_next(B1, 3)
    u_relay(4)
    s_end(2, 1)
    convert_many(2, lambda i: (lax.rem(x + 2, NX) * NZL + 1 - zl, i))
    pairs = [(y_of(d), y_of(8 - d)) for d in range(1, 4)] + [(y, y_of(4))]
    for k in range(2):
        for i in range(3):
            forward(pairs[i], k, i == 0)
    for i in range(3):
        u_end(i + 1)
        u_end(7 - i)
        forward(pairs[i], 2, i == 0)
    y_end(A, 4)
    y_end(B0, 4)
    forward(pairs[3], 0)
    y_end(B1, 4)
    forward(pairs[3], 1)
    u_end(0)
    u_end(4)
    forward(pairs[3], 2)

    def rows_body(r, carry):
        rows = pl.ds(pl.multiple_of(r * 64, 64), 64)
        back = acc[0, rows, :]
        gate = acc[1, rows, :]
        lift = acc[2, rows, :]
        s = 1.0 / (1.0 + jnp.exp(-gate))
        bs = back * s
        hi, lo = split(bs * lift * (1.0 + gate * (1.0 - s)))
        rh[rows, 0:256] = hi
        rl[rows, 0:256] = lo
        hi, lo = split(bs * gate)
        rh[rows, 256:512] = hi
        rl[rows, 256:512] = lo
        return carry

    lax.fori_loop(0, 8, rows_body, 0)

    def backward(bs):
        h = jnp.concatenate([xth[b] for b in bs], axis=0) if len(bs) == 2 else xth[bs[0]]
        l = jnp.concatenate([xtl[b] for b in bs], axis=0) if len(bs) == 2 else xtl[bs[0]]
        v = dot3(h, l, rh[:, 0:384], rl[:, 0:384])
        for i, b in enumerate(bs):
            for q in range(3):
                gbuf[b, q] = v[i * 128 : (i + 1) * 128, q * 128 : (q + 1) * 128]

    def backward_last(i, carry):
        h = jnp.concatenate([xth[2 * i], xth[2 * i + 1]], axis=0)
        l = jnp.concatenate([xtl[2 * i], xtl[2 * i + 1]], axis=0)
        v = dot3(h, l, rh[:, 384:512], rl[:, 384:512])
        gz[2 * i] = v[0:128]
        gz[2 * i + 1] = v[128:256]
        return carry

    def r_start(s, q, d):
        b = y_of(5 - s) if d == 0 else y_of(3 + s)
        rows = pl.ds(64 * d, 64) if s == 1 else pl.ds(0, 128)
        remote(
            gbuf.at[b, q, rows, :], rbuf.at[d, s - 1, q, rows, :],
            r_send.at[d, s - 1, q], r_recv.at[d, s - 1, q], ys[d],
        )

    def r_step(s):
        for q in range(3):
            for d in range(2):
                b = y_of(5 - s) if d == 0 else y_of(3 + s)
                rows = pl.ds(64 * d, 64) if s == 2 else pl.ds(0, 128)
                wait(rbuf.at[d, s - 2, q, rows, :], r_recv.at[d, s - 2, q])
                gbuf[b, q, rows, :] += rbuf[d, s - 2, q, rows, :]
                r_start(s, q, d)

    def z_rows(d, first, n):
        return pl.ds(pl.multiple_of(zat[d] * 32 + first, 16), n)

    backward((y_of(4),))
    for q in range(3):
        for d in range(2):
            r_start(1, q, d)
    lax.fori_loop(0, 4, backward_last, 0)
    for d in range(2):
        remote(gz.at[:, z_rows(2, 16 * d, 16), :], rz1.at[d], f_send.at[0, d], f_recv.at[0, d], zs[d])
    backward((y_of(3), y_of(5)))
    r_step(2)
    backward((y_of(2), y_of(6)))
    for d, dz in ((0, 1), (1, 3)):
        wait(rz1.at[d], f_recv.at[0, d])
        rows = z_rows(dz, 16 * d, 16)
        gz[:, rows, :] = gz[:, rows, :] + rz1[d]
        remote(gz.at[:, z_rows(dz, 0, 32), :], rz2.at[d], f_send.at[1, d], f_recv.at[1, d], zs[d])
    r_step(3)
    backward((y_of(1), y_of(7)))
    r_step(4)
    backward((y,))
    for d in range(2):
        wait(rz2.at[d], f_recv.at[1, d])
    rows = z_rows(0, 0, 32)
    gz[:, rows, :] = gz[:, rows, :] + rz2[0] + rz2[1]
    for dy, dc in ypeers + [(0, 1)]:
        rows = pl.ds(pl.multiple_of(zh * 32 + core_of(dc) * 16, 16), 16)
        remote(gz.at[y_of(dy), rows, :], yz.at[y * 2 + c], g_send, g_recv, dev_of(dy, 0, dc))
    yz[y * 2 + c] = gz[y, pl.ds(pl.multiple_of(zh * 32 + c * 16, 16), 16), :]

    src = zh * 2 + c
    for q in range(3):
        for d in range(2):
            wait(rbuf.at[d, 3, q], r_recv.at[d, 3, q])
        for i in range(8):
            rows = pl.ds(16 * i, 16)
            tbuf[q, i] = gbuf[y, q, rows, :] + rbuf[0, 3, q, rows, :] + rbuf[1, 3, q, rows, :]
        for dz, dc in zpeers + [(0, 1)]:
            remote(
                tbuf.at[q, zat[dz] * 2 + core_of(dc)], zbuf.at[q, src],
                z_send.at[q], z_recv.at[q], dev_of(0, dz, dc),
            )
        zbuf[q, src] = tbuf[q, src]
    wait(yz.at[pl.ds(0, 15)], g_recv)
    for cc in range(2):
        v = yz[cc]
        for i in range(1, NY):
            v = v + yz[2 * i + cc]
        out_ref[1, :, cc * 256 + 128 : cc * 256 + 256] = v
    for q in range(3):
        wait(zbuf.at[q, pl.ds(0, 7)], z_recv.at[q])
        for cc in range(2):
            col = cc * 256 + (q % 2) * 128
            out_ref[q // 2, :, col : col + 128] = (
                (zbuf[q, cc] + zbuf[q, 2 + cc]) + (zbuf[q, 4 + cc] + zbuf[q, 6 + cc])
            )

    def sent(rows, sem):
        wait(w.at[0, 0, pl.ds(0, rows), :], sem)

    sent(32, o_send.at[0])
    sent(16, o_send.at[1])
    sent(96, w_send.at[0])
    sent(96, w_send.at[1])
    for n in range(14):
        sent(128, a_send.at[n])
    for dx in range(4):
        for dz in range(2):
            wait(xc.at[0, 0], s_send.at[dx, dz])
    for d in range(2):
        for s in range(4):
            for ring, rows in ((U, 32), (A, 64), (B0, 96), (B1, 96)):
                sent(rows // 2 if s == 3 else rows, y_send.at[d, s, ring])
            for q in range(3):
                sent(32 if s == 0 else 64, r_send.at[d, s, q])
        for i in range(NY):
            sent(32, u_send.at[0, d, i])
            sent(16, u_send.at[1, d, i])
        sent(64, f_send.at[0, d])
        sent(128, f_send.at[1, d])
    for q in range(3):
        sent(56, z_send.at[q])
    sent(120, g_send)


def grads(inputs, cotangent, gate_weight, up_weight, down_weight):
    dma = pltpu.SemaphoreType.DMA
    return pl.pallas_call(
        kernel,
        name="grads",
        out_shape=jax.ShapeDtypeStruct((2, 16, 512), F32),
        in_specs=[pl.BlockSpec(memory_space=pl.ANY)] * 5,
        out_specs=pl.BlockSpec(memory_space=pltpu.VMEM),
        scratch_shapes=[
            pltpu.VMEM((8, 2, 2, 256, 128), F32),
            pltpu.VMEM((8, 3, 128, 256), F32),
            pltpu.VMEM((8, 512, 128), BF16),
            pltpu.VMEM((8, 512, 128), BF16),
            pltpu.VMEM((8, 512, 128), BF16),
            pltpu.VMEM((8, 512, 128), BF16),
            pltpu.VMEM((8, 128, 512), BF16),
            pltpu.VMEM((8, 128, 512), BF16),
            pltpu.VMEM((3, 512, 256), F32),
            pltpu.VMEM((512, 512), BF16),
            pltpu.VMEM((512, 512), BF16),
            pltpu.VMEM((8, 3, 128, 128), F32),
            pltpu.VMEM((2, 4, 3, 128, 128), F32),
            pltpu.VMEM((3, 8, 16, 128), F32),
            pltpu.VMEM((3, 8, 16, 128), F32),
            pltpu.VMEM((8, 128, 128), F32),
            pltpu.VMEM((2, 8, 16, 128), F32),
            pltpu.VMEM((2, 8, 32, 128), F32),
            pltpu.VMEM((16, 16, 128), F32),
            dma,
            dma((4, 2, 2)),
            dma((14,)),
            dma((4, 2)),
            dma((4, 2)),
            dma((2,)),
            dma((2,)),
            dma((2,)),
            dma((2,)),
            dma((2, 4, 4)),
            dma((2, 4, 4)),
            dma((2, 2, 8)),
            dma((2, 2, 8)),
            dma((2, 4, 3)),
            dma((2, 4, 3)),
            dma((3,)),
            dma((3,)),
            dma((2, 2)),
            dma((2, 2)),
            dma,
            dma,
        ],
        compiler_params=pltpu.CompilerParams(
            collective_id=0, has_side_effects=True, vmem_limit_bytes=66400000
        ),
    )(inputs, cotangent, gate_weight, up_weight, down_weight)


def local(
    inputs,
    cotangent,
    gate_weight,
    up_weight,
    down_weight,
    gate_first,
    gate_second,
    up_first,
    up_second,
):
    g = grads(inputs, cotangent, gate_weight, up_weight, down_weight)
    gate_new, gate_first_new, gate_second_new = adam_update(
        gate_weight, gate_first, gate_second, g[0]
    )
    up_new, up_first_new, up_second_new = adam_update(up_weight, up_first, up_second, g[1])
    return (gate_new, gate_first_new, gate_second_new, up_new, up_first_new, up_second_new)


def solution(mesh):
    spec = P("dp", "tensor")
    return jax.shard_map(
        local, mesh=mesh, in_specs=(spec,) * 9, out_specs=(spec,) * 6, check_vma=False
    )
```

```python
import jax
import jax.numpy as jnp
from jax import lax
from jax.experimental import pallas as pl
from jax.experimental.pallas import tpu as pltpu
from jax.sharding import PartitionSpec as P

STEP = 100
MESH = pl.DeviceIdType.MESH
F32 = jnp.float32
BF16 = jnp.bfloat16
NX, NZL, NY, NZH = 4, 2, 8, 4


def adam_update(weight, first, second, grad):
    first_new = 0.9 * first + 0.1 * grad
    second_new = 0.95 * second + 0.05 * grad * grad
    first_hat = first_new / (1.0 - 0.9**STEP)
    second_hat = second_new / (1.0 - 0.95**STEP)
    weight_new = weight - 0.003 * first_hat / (jnp.sqrt(second_hat) + 1e-08)
    return (weight_new, first_new, second_new)


def split(v):
    hi = v.astype(BF16)
    return hi, (v - hi.astype(F32)).astype(BF16)


def dot(a, b):
    return jnp.dot(a, b, preferred_element_type=F32)


def dot3(ah, al, bh, bl):
    return dot(ah, bh) + dot(ah, bl) + dot(al, bh)


def kernel(
    in_ref, cot_ref, gw_ref, uw_ref, dw_ref, out_ref,
    xc, w, xh, xl, ch, cl, xth, xtl, acc, rh, rl,
    gbuf, rbuf, tbuf, zbuf, gz, rz1, rz2, yz,
    counted, sent, own_sem, a_recv, s_recv, o_recv, w_recv, y_recv, u_recv, r_recv, z_recv, f_recv, g_recv,
):
    dp = lax.axis_index("dp")
    t = lax.axis_index("tensor")
    c = lax.rem(dp, 2)
    zh = lax.rem(dp // 2, NZH)
    y = dp // (2 * NZH)
    x = t // NZL
    zl = lax.rem(t, NZL)

    def t_of(dx, dz):
        zz = zl if dz == 0 else 1 - zl
        return lax.rem(x + dx, NX) * NZL + zz

    def y_of(d):
        return lax.rem(y + d, NY)

    def core_of(dc):
        return c if dc == 0 else 1 - c

    def dev_of(dy, dz, dc):
        return ((y_of(dy) * NZH + zat[dz]) * 2 + core_of(dc), t)

    zat = [lax.rem(zh + d, NZH) for d in range(NZH)]
    sib = dev_of(0, 0, 1)
    zpart = (dp, t_of(0, 1))
    xs = ((dp, t_of(1, 0)), (dp, t_of(3, 0)))
    ys = (dev_of(1, 0, 0), dev_of(7, 0, 0))
    zs = (dev_of(0, 1, 0), dev_of(0, 3, 0))
    zpeers = [(2, 0), (2, 1), (1, 0), (3, 0), (1, 1), (3, 1)]
    ypeers = [(dy, dc) for dy in (4, 3, 5, 2, 6, 1, 7) for dc in range(2)]

    barrier = pltpu.get_barrier_semaphore()
    peers = [dev_of(0, dz, dc) for dz, dc in zpeers] + [sib, zpart, xs[0], xs[1]]
    peers = peers + [dev_of(dy, 0, dc) for dy, dc in ypeers]
    for peer in peers:
        pl.semaphore_signal(barrier, inc=1, device_id=peer, device_id_type=MESH)
    pl.semaphore_wait(barrier, len(peers))

    sent_rows = [0, 0, 0]

    def remote(src, dst, group, recv, dev):
        n = 1
        for extent in src.shape:
            n = n * extent
        sent_rows[group] += n // 128
        pltpu.make_async_remote_copy(
            src_ref=src, dst_ref=dst, send_sem=sent.at[group], recv_sem=recv,
            device_id=dev, device_id_type=MESH,
        ).start()

    def local_copy(src, dst, sem):
        pltpu.make_async_copy(src, dst, sem).start()

    def wait(ref, sem):
        pltpu.make_async_copy(ref, ref, sem).wait()

    w_srcs = (dw_ref, gw_ref, uw_ref)

    def w_own(k):
        mine = pl.ds(pl.multiple_of(c * 16, 16), 16)
        there = pl.ds(pl.multiple_of((1 - c) * 256, 256), 256)
        remote(w_srcs[k].at[:, there], w.at[y, k, mine, :], 1, o_recv.at[k // 2], sib)
        here = pl.ds(pl.multiple_of(c * 256, 256), 256)
        local_copy(w_srcs[k].at[:, here], w.at[y, k, mine, :], o_recv.at[k // 2])

    def w_first(k):
        for dz, dc in zpeers:
            src = w_srcs[k].at[:, pl.ds(pl.multiple_of(core_of(dc) * 256, 256), 256)]
            rows = pl.ds(pl.multiple_of((4 - dz) * 32 + c * 16, 16), 16)
            remote(src, w.at[y, k, rows, :], 1, w_recv.at[k], dev_of(0, dz, dc))

    U, A, B0, B1 = range(4)

    def part(ring, b, half):
        if ring == A:
            return w.at[b, pl.ds(0, 2), pl.ds(0, 32), :] if half is None else w.at[b, half, pl.ds(0, 32), :]
        k = (2, 0, 0, 1)[ring]
        first, n = (0, 32) if ring == U else (32, 96)
        if half is not None:
            n = n // 2
            first = first + half * n
        return w.at[b, k, pl.ds(first, n), :]

    def step_parts(ring, s, back):
        if s < 4:
            return part(ring, y_of((9 - s - back) % 8), None), part(ring, y_of(s - 1 + back), None)
        return part(ring, y_of(5 - back), 0), part(ring, y_of(3 + back), 1)

    def y_start(ring, s):
        for d, r in enumerate(step_parts(ring, s, 0)):
            remote(r, r, 1, y_recv.at[d, s - 1, ring], ys[d])

    def y_end(ring, s):
        for d, r in enumerate(step_parts(ring, s, 1)):
            wait(r, y_recv.at[d, s - 1, ring])

    def y_next(ring, s):
        y_end(ring, s)
        y_start(ring, s + 1)

    def z_start(i):
        b = y_of(i)
        for d, first in enumerate((96, 32)):
            remote(
                w.at[b, 2, pl.ds(0, 32), :], w.at[b, 2, pl.ds(first, 32), :],
                1, u_recv.at[0, d, i], zs[d],
            )

    def z_relay(i):
        b = y_of(i)
        for d, (first, src, dst) in enumerate(((96, 96, 64), (32, 48, 80))):
            wait(w.at[b, 2, pl.ds(first, 32), :], u_recv.at[0, d, i])
            remote(
                w.at[b, 2, pl.ds(src, 16), :], w.at[b, 2, pl.ds(dst, 16), :],
                1, u_recv.at[1, d, i], zs[d],
            )

    def z_end(i):
        for d in range(2):
            wait(w.at[y_of(i), 2, pl.ds(64 + 16 * d, 16), :], u_recv.at[1, d, i])

    own = t_of(0, 0)
    rows_src = (in_ref, cot_ref)

    def own_to(n, j, dev, recv):
        remote(rows_src[j], xc.at[own, c, j], 0, recv, dev)

    def pass_on(n, dx, dz, j, d, to_dx):
        b = xc.at[t_of(dx, dz), c, j]
        remote(b, b, 0, a_recv.at[to_dx, dz, j], xs[d])

    def a_end(dx, dz, j):
        wait(xc.at[t_of(dx, dz), c, j], a_recv.at[dx, dz, j])

    def from_right(dz):
        a_end(1, dz, 1)
        pass_on(10 + dz, 1, dz, 1, 1, 2)

    def from_left(dz):
        a_end(3, dz, 0)
        pass_on(12 + dz, 3, dz, 0, 0, 2)

    def to_sibling(dx, dz):
        b = xc.at[t_of(dx, dz), c]
        remote(b, b, 0, s_recv.at[dx, dz], sib)

    def s_end(dx, dz):
        wait(xc.at[t_of(dx, dz), 1 - c], s_recv.at[dx, dz])

    def convert(tt, cc):
        rows = pl.ds(pl.multiple_of(cc * 256, 256), 256)
        v = xc[tt, cc, 0]
        hi, lo = split(v)
        xh[tt, rows, :] = hi
        xl[tt, rows, :] = lo
        hi, lo = split(jnp.transpose(v))
        xth[tt, :, rows] = hi
        xtl[tt, :, rows] = lo
        hi, lo = split(xc[tt, cc, 1])
        ch[tt, rows, :] = hi
        cl[tt, rows, :] = lo

    def convert_many(n, where):
        def body(i, carry):
            convert(*where(i))
            return carry

        lax.fori_loop(0, n, body, 0)

    lhs = ((ch, cl), (xh, xl), (xh, xl))
    w_rows = [pl.ds(pl.multiple_of(lax.rem(j + NZH - zh, NZH) * 32, 32), 32) for j in range(NZH)]

    def forward(bs, k, first=False):
        wh, wl = split(jnp.concatenate([w[b, k, r, :] for b in bs for r in w_rows], axis=0))
        ah, al = lhs[k]
        if len(bs) == 2:
            h = jnp.concatenate([ah[b] for b in bs], axis=1)
            l = jnp.concatenate([al[b] for b in bs], axis=1)
        else:
            h, l = ah[bs[0]], al[bs[0]]
        v = dot3(h, l, wh, wl)
        if first:
            acc[k] = v
        else:
            acc[k] += v

    w_own(2)
    w_own(0)
    w_own(1)
    for j in range(2):
        own_to(0, j, xs[0], a_recv.at[3, 0, j])
        own_to(2, j, xs[1], a_recv.at[1, 0, j])
    w_first(0)
    w_first(1)
    for j in range(2):
        own_to(4, j, zpart, a_recv.at[0, 1, j])
    for j in range(2):
        remote(rows_src[j], xc.at[own, c, j], 0, s_recv.at[0, 0], sib)
        local_copy(rows_src[j], xc.at[own, c, j], own_sem)

    wait(part(U, y, None), o_recv.at[1])
    y_start(U, 1)
    z_start(0)
    wait(part(A, y, None), o_recv.at[0])
    y_start(A, 1)
    y_next(U, 1)
    z_start(1)
    z_start(7)
    y_next(A, 1)
    y_next(U, 2)
    z_start(2)
    z_start(6)
    from_left(0)
    wait(part(B0, y, None), w_recv.at[0])
    y_start(B0, 1)
    from_right(0)
    a_end(1, 0, 0)
    to_sibling(1, 0)
    a_end(3, 0, 1)
    to_sibling(3, 0)
    y_next(A, 2)
    y_next(U, 3)
    z_start(3)
    z_start(5)
    wait(part(B1, y, None), w_recv.at[1])
    y_start(B1, 1)
    a_end(0, 1, 0)
    pass_on(6, 0, 1, 0, 0, 3)
    pass_on(8, 0, 1, 0, 1, 1)
    y_next(B0, 1)
    for j in range(2):
        a_end(2, 0, j)
    to_sibling(2, 0)
    y_next(A, 3)
    y_end(U, 4)
    z_start(4)
    y_next(B1, 1)
    a_end(0, 1, 1)
    pass_on(9, 0, 1, 1, 1, 1)
    pass_on(7, 0, 1, 1, 0, 3)
    to_sibling(0, 1)
    y_next(B0, 2)
    wait(xc.at[own, c], own_sem)
    s_end(0, 0)
    s_end(1, 0)
    s_end(3, 0)
    convert_many(6, lambda i: (lax.rem(x + 3 + i // 2, NX) * NZL + zl, lax.rem(i, 2)))
    from_left(1)
    z_relay(0)
    y_next(B1, 2)
    s_end(2, 0)
    convert_many(2, lambda i: (lax.rem(x + 2, NX) * NZL + zl, i))
    s_end(0, 1)
    convert_many(2, lambda i: (x * NZL + 1 - zl, i))
    from_right(1)
    a_end(1, 1, 0)
    to_sibling(1, 1)
    a_end(3, 1, 1)
    to_sibling(3, 1)
    y_next(B0, 3)
    z_relay(1)
    z_relay(7)
    z_relay(2)
    z_relay(6)
    for j in range(2):
        a_end(2, 1, j)
    to_sibling(2, 1)
    y_next(B1, 3)
    s_end(1, 1)
    s_end(3, 1)
    convert_many(4, lambda i: (lax.rem(x + 3 + 2 * (i // 2), NX) * NZL + 1 - zl, lax.rem(i, 2)))
    z_relay(3)
    z_relay(5)
    z_relay(4)
    s_end(2, 1)
    convert_many(2, lambda i: (lax.rem(x + 2, NX) * NZL + 1 - zl, i))
    pairs = [(y_of(d), y_of(8 - d)) for d in range(1, 4)] + [(y, y_of(4))]
    for k in range(2):
        for i in range(3):
            forward(pairs[i], k, i == 0)
    y_end(A, 4)
    y_end(B0, 4)
    y_end(B1, 4)
    for k in range(2):
        forward(pairs[3], k)

    def grad_rows(m):
        def body(r, carry):
            rows = pl.ds(pl.multiple_of(r * 64, 64), 64)
            gate = acc[1, rows, :]
            s = 1.0 / (1.0 + jnp.exp(-gate))
            bs = acc[0, rows, :] * s
            v = bs * gate if m == 1 else bs * acc[2, rows, :] * (1.0 + gate * (1.0 - s))
            hi, lo = split(v)
            rh[m, rows, :] = hi
            rl[m, rows, :] = lo
            return carry

        lax.fori_loop(0, 8, body, 0)

    def backward(bs, m):
        h = jnp.concatenate([xth[b] for b in bs], axis=0)
        l = jnp.concatenate([xtl[b] for b in bs], axis=0)
        v = dot3(h, l, rh[m], rl[m])
        for i, b in enumerate(bs):
            rows = slice(i * 128, i * 128 + 128)
            gbuf[b, 2 * m] = v[rows, 0:128]
            if m == 0:
                gbuf[b, 1] = v[rows, 128:256]
            else:
                gz[b] = v[rows, 128:256]

    def r_start(s, q, d):
        b = y_of(5 - s) if d == 0 else y_of(3 + s)
        rows = pl.ds(64 * d, 64) if s == 1 else pl.ds(0, 128)
        remote(
            gbuf.at[b, q, rows, :], rbuf.at[d, s - 1, q, rows, :],
            2, r_recv.at[d, s - 1, q], ys[d],
        )

    def r_step(s, *qs):
        for q in qs:
            for d in range(2):
                if s == 1:
                    r_start(s, q, d)
                    continue
                b = y_of(5 - s) if d == 0 else y_of(3 + s)
                rows = pl.ds(64 * d, 64) if s == 2 else pl.ds(0, 128)
                wait(rbuf.at[d, s - 2, q, rows, :], r_recv.at[d, s - 2, q])
                gbuf[b, q, rows, :] += rbuf[d, s - 2, q, rows, :]
                r_start(s, q, d)

    def r_end(q):
        for d in range(2):
            wait(rbuf.at[d, 3, q], r_recv.at[d, 3, q])
        for i in range(8):
            rows = pl.ds(16 * i, 16)
            tbuf[q, i] = gbuf[y, q, rows, :] + rbuf[0, 3, q, rows, :] + rbuf[1, 3, q, rows, :]
        src = zh * 2 + c
        for dz, dc in zpeers + [(0, 1)]:
            remote(
                tbuf.at[q, zat[dz] * 2 + core_of(dc)], zbuf.at[q, src],
                2, z_recv.at[q], dev_of(0, dz, dc),
            )
        zbuf[q, src] = tbuf[q, src]

    def z_rows(d, first, n):
        return pl.ds(pl.multiple_of(zat[d] * 32 + first, 16), n)

    grad_rows(1)
    backward(pairs[3], 1)
    r_step(1, 2)
    for i in range(3):
        z_end(i + 1)
        z_end(7 - i)
    for i in range(3):
        forward(pairs[i], 2, i == 0)
    z_end(0)
    z_end(4)
    forward(pairs[3], 2)
    grad_rows(0)
    backward(pairs[3], 0)
    r_step(1, 0, 1)
    for i in (2, 1, 0):
        backward(pairs[i], 1)
    for d in range(2):
        remote(gz.at[:, z_rows(2, 16 * d, 16), :], rz1.at[d], 2, f_recv.at[0, d], zs[d])
    r_step(2, 2)
    backward(pairs[2], 0)
    r_step(2, 0, 1)
    r_step(3, 2)
    for d, dz in ((0, 1), (1, 3)):
        wait(rz1.at[d], f_recv.at[0, d])
        rows = z_rows(dz, 16 * d, 16)
        gz[:, rows, :] = gz[:, rows, :] + rz1[d]
        remote(gz.at[:, z_rows(dz, 0, 32), :], rz2.at[d], 2, f_recv.at[1, d], zs[d])
    backward(pairs[1], 0)
    r_step(3, 0, 1)
    backward(pairs[0], 0)
    r_step(4, 2)
    r_step(4, 0, 1)
    r_end(2)
    for d in range(2):
        wait(rz2.at[d], f_recv.at[1, d])
    rows = z_rows(0, 0, 32)
    gz[:, rows, :] = gz[:, rows, :] + rz2[0] + rz2[1]
    for dy, dc in ypeers + [(0, 1)]:
        rows = pl.ds(pl.multiple_of(zh * 32 + core_of(dc) * 16, 16), 16)
        remote(gz.at[y_of(dy), rows, :], yz.at[y * 2 + c], 2, g_recv, dev_of(dy, 0, dc))
    yz[y * 2 + c] = gz[y, pl.ds(pl.multiple_of(zh * 32 + c * 16, 16), 16), :]
    r_end(0)
    r_end(1)
    wait(yz.at[pl.ds(0, 15)], g_recv)
    for cc in range(2):
        v = yz[cc]
        for i in range(1, NY):
            v = v + yz[2 * i + cc]
        out_ref[1, :, cc * 256 + 128 : cc * 256 + 256] = v
    for q in (2, 0, 1):
        wait(zbuf.at[q, pl.ds(0, 7)], z_recv.at[q])
        for cc in range(2):
            col = cc * 256 + (q % 2) * 128
            out_ref[q // 2, :, col : col + 128] = (
                (zbuf[q, cc] + zbuf[q, 2 + cc]) + (zbuf[q, 4 + cc] + zbuf[q, 6 + cc])
            )

    for group in range(3):
        wait(counted.at[pl.ds(0, sent_rows[group]), :], sent.at[group])


def grads(inputs, cotangent, gate_weight, up_weight, down_weight):
    dma = pltpu.SemaphoreType.DMA
    return pl.pallas_call(
        kernel,
        name="grads",
        out_shape=jax.ShapeDtypeStruct((2, 16, 512), F32),
        in_specs=[pl.BlockSpec(memory_space=pl.ANY)] * 5,
        out_specs=pl.BlockSpec(memory_space=pltpu.VMEM),
        scratch_shapes=[
            pltpu.VMEM((8, 2, 2, 256, 128), F32),
            pltpu.VMEM((8, 3, 128, 256), F32),
            pltpu.VMEM((8, 512, 128), BF16),
            pltpu.VMEM((8, 512, 128), BF16),
            pltpu.VMEM((8, 512, 128), BF16),
            pltpu.VMEM((8, 512, 128), BF16),
            pltpu.VMEM((8, 128, 512), BF16),
            pltpu.VMEM((8, 128, 512), BF16),
            pltpu.VMEM((3, 512, 256), F32),
            pltpu.VMEM((2, 512, 256), BF16),
            pltpu.VMEM((2, 512, 256), BF16),
            pltpu.VMEM((8, 3, 128, 128), F32),
            pltpu.VMEM((2, 4, 3, 128, 128), F32),
            pltpu.VMEM((3, 8, 16, 128), F32),
            pltpu.VMEM((3, 8, 16, 128), F32),
            pltpu.VMEM((8, 128, 128), F32),
            pltpu.VMEM((2, 8, 16, 128), F32),
            pltpu.VMEM((2, 8, 32, 128), F32),
            pltpu.VMEM((16, 16, 128), F32),
            pltpu.VMEM((8192, 128), F32),
            dma((3,)),
            dma,
            dma((4, 2, 2)),
            dma((4, 2)),
            dma((2,)),
            dma((2,)),
            dma((2, 4, 4)),
            dma((2, 2, 8)),
            dma((2, 4, 3)),
            dma((3,)),
            dma((2, 2)),
            dma,
        ],
        compiler_params=pltpu.CompilerParams(
            collective_id=0, has_side_effects=True, vmem_limit_bytes=66400000
        ),
    )(inputs, cotangent, gate_weight, up_weight, down_weight)


def local(
    inputs,
    cotangent,
    gate_weight,
    up_weight,
    down_weight,
    gate_first,
    gate_second,
    up_first,
    up_second,
):
    g = grads(inputs, cotangent, gate_weight, up_weight, down_weight)
    gate_new, gate_first_new, gate_second_new = adam_update(
        gate_weight, gate_first, gate_second, g[0]
    )
    up_new, up_first_new, up_second_new = adam_update(up_weight, up_first, up_second, g[1])
    return (gate_new, gate_first_new, gate_second_new, up_new, up_first_new, up_second_new)


def solution(mesh):
    spec = P("dp", "tensor")
    return jax.shard_map(
        local, mesh=mesh, in_specs=(spec,) * 9, out_specs=(spec,) * 6, check_vma=False
    )
```

```python
import jax
import jax.numpy as jnp
from jax import lax
from jax.experimental import pallas as pl
from jax.experimental.pallas import tpu as pltpu
from jax.sharding import PartitionSpec as P

STEP = 100
MESH = pl.DeviceIdType.MESH
F32 = jnp.float32
BF16 = jnp.bfloat16
NX, NZL, NY, NZH = 4, 2, 8, 4


def adam_update(weight, first, second, grad):
    first_new = 0.9 * first + 0.1 * grad
    second_new = 0.95 * second + 0.05 * grad * grad
    first_hat = first_new / (1.0 - 0.9**STEP)
    second_hat = second_new / (1.0 - 0.95**STEP)
    weight_new = weight - 0.003 * first_hat / (jnp.sqrt(second_hat) + 1e-08)
    return (weight_new, first_new, second_new)


def split(v):
    hi = v.astype(BF16)
    return hi, (v - hi.astype(F32)).astype(BF16)


def dot(a, b):
    return jnp.dot(a, b, preferred_element_type=F32)


def dot3(ah, al, bh, bl):
    return dot(ah, bh) + dot(ah, bl) + dot(al, bh)


def kernel(
    in_ref, cot_ref, gw_ref, uw_ref, dw_ref, out_ref,
    xc, w, xh, xl, ch, cl, xth, xtl, acc, rh, rl,
    gbuf, rbuf, tbuf, zbuf, gz, rz1, rz2, yz,
    counted, sent, own_sem, a_recv, s_recv, o_recv, w_recv, y_recv, u_recv, r_recv, z_recv, f_recv, g_recv,
):
    dp = lax.axis_index("dp")
    t = lax.axis_index("tensor")
    c = lax.rem(dp, 2)
    zh = lax.rem(dp // 2, NZH)
    y = dp // (2 * NZH)
    x = t // NZL
    zl = lax.rem(t, NZL)

    def t_of(dx, dz):
        zz = zl if dz == 0 else 1 - zl
        return lax.rem(x + dx, NX) * NZL + zz

    def y_of(d):
        return lax.rem(y + d, NY)

    def core_of(dc):
        return c if dc == 0 else 1 - c

    def dev_of(dy, dz, dc):
        return ((y_of(dy) * NZH + zat[dz]) * 2 + core_of(dc), t)

    zat = [lax.rem(zh + d, NZH) for d in range(NZH)]
    sib = dev_of(0, 0, 1)
    zpart = (dp, t_of(0, 1))
    xs = ((dp, t_of(1, 0)), (dp, t_of(3, 0)))
    ys = (dev_of(1, 0, 0), dev_of(7, 0, 0))
    zs = (dev_of(0, 1, 0), dev_of(0, 3, 0))
    zpeers = [(2, 0), (2, 1), (1, 0), (3, 0), (1, 1), (3, 1)]
    ypeers = [(dy, dc) for dy in (4, 3, 5, 2, 6, 1, 7) for dc in range(2)]

    barrier = pltpu.get_barrier_semaphore()
    peers = [dev_of(0, dz, dc) for dz, dc in zpeers] + [sib, zpart, xs[0], xs[1]]
    peers = peers + [dev_of(dy, 0, dc) for dy, dc in ypeers]
    for peer in peers:
        pl.semaphore_signal(barrier, inc=1, device_id=peer, device_id_type=MESH)
    pl.semaphore_wait(barrier, len(peers))

    sent_rows = [0, 0, 0]

    def remote(src, dst, group, recv, dev):
        n = 1
        for extent in src.shape:
            n = n * extent
        sent_rows[group] += n // 128
        pltpu.make_async_remote_copy(
            src_ref=src, dst_ref=dst, send_sem=sent.at[group], recv_sem=recv,
            device_id=dev, device_id_type=MESH,
        ).start()

    def local_copy(src, dst, sem):
        pltpu.make_async_copy(src, dst, sem).start()

    def wait(ref, sem):
        pltpu.make_async_copy(ref, ref, sem).wait()

    def wait_rows(n, sem):
        wait(counted.at[pl.ds(0, n), :], sem)

    w_srcs = (dw_ref, gw_ref, uw_ref)

    def w_own(k):
        mine = pl.ds(pl.multiple_of(c * 16, 16), 16)
        there = pl.ds(pl.multiple_of((1 - c) * 256, 256), 256)
        remote(w_srcs[k].at[:, there], w.at[y, k, mine, :], 1, o_recv.at[k // 2], sib)
        here = pl.ds(pl.multiple_of(c * 256, 256), 256)
        local_copy(w_srcs[k].at[:, here], w.at[y, k, mine, :], o_recv.at[k // 2])

    def w_first(k):
        for dz, dc in zpeers:
            src = w_srcs[k].at[:, pl.ds(pl.multiple_of(core_of(dc) * 256, 256), 256)]
            rows = pl.ds(pl.multiple_of((4 - dz) * 32 + c * 16, 16), 16)
            remote(src, w.at[y, k, rows, :], 1, w_recv.at[k], dev_of(0, dz, dc))

    U, A, B0, B1 = range(4)

    def part(ring, b, half):
        if ring == A:
            return w.at[b, pl.ds(0, 2), pl.ds(0, 32), :] if half is None else w.at[b, half, pl.ds(0, 32), :]
        k = (2, 0, 0, 1)[ring]
        first, n = (0, 32) if ring == U else (32, 96)
        if half is not None:
            n = n // 2
            first = first + half * n
        return w.at[b, k, pl.ds(first, n), :]

    def step_parts(ring, s, back):
        if s < 4:
            return part(ring, y_of((9 - s - back) % 8), None), part(ring, y_of(s - 1 + back), None)
        return part(ring, y_of(5 - back), 0), part(ring, y_of(3 + back), 1)

    def y_start(ring, s):
        for d, r in enumerate(step_parts(ring, s, 0)):
            remote(r, r, 1, y_recv.at[s - 1, ring], ys[d])

    def y_end(ring, s):
        wait_rows((128, 256, 384, 384)[ring] // (2 if s == 4 else 1), y_recv.at[s - 1, ring])

    def y_next(ring, s):
        y_end(ring, s)
        y_start(ring, s + 1)

    def z_start(i):
        b = y_of(i)
        for d, first in enumerate((96, 32)):
            remote(w.at[b, 2, pl.ds(0, 32), :], w.at[b, 2, pl.ds(first, 32), :], 1, u_recv.at[0, i], zs[d])

    def z_relay(i):
        b = y_of(i)
        wait_rows(128, u_recv.at[0, i])
        for d, (src, dst) in enumerate(((96, 64), (48, 80))):
            remote(w.at[b, 2, pl.ds(src, 16), :], w.at[b, 2, pl.ds(dst, 16), :], 1, u_recv.at[1, i], zs[d])

    def z_end(i):
        wait_rows(64, u_recv.at[1, i])

    own = t_of(0, 0)
    rows_src = (in_ref, cot_ref)

    def own_to(n, j, dev, recv):
        remote(rows_src[j], xc.at[own, c, j], 0, recv, dev)

    def pass_on(n, dx, dz, j, d, to_dx):
        b = xc.at[t_of(dx, dz), c, j]
        remote(b, b, 0, a_recv.at[to_dx, dz, j], xs[d])

    def a_end(dx, dz, j):
        wait(xc.at[t_of(dx, dz), c, j], a_recv.at[dx, dz, j])

    def from_right(dz):
        a_end(1, dz, 1)
        pass_on(10 + dz, 1, dz, 1, 1, 2)

    def from_left(dz):
        a_end(3, dz, 0)
        pass_on(12 + dz, 3, dz, 0, 0, 2)

    def to_sibling(dx, dz):
        b = xc.at[t_of(dx, dz), c]
        remote(b, b, 0, s_recv.at[dx, dz], sib)

    def s_end(dx, dz):
        wait(xc.at[t_of(dx, dz), 1 - c], s_recv.at[dx, dz])

    def convert(tt, cc):
        rows = pl.ds(pl.multiple_of(cc * 256, 256), 256)
        v = xc[tt, cc, 0]
        hi, lo = split(v)
        xh[tt, rows, :] = hi
        xl[tt, rows, :] = lo
        hi, lo = split(jnp.transpose(v))
        xth[tt, :, rows] = hi
        xtl[tt, :, rows] = lo
        hi, lo = split(xc[tt, cc, 1])
        ch[tt, rows, :] = hi
        cl[tt, rows, :] = lo

    def convert_many(n, where):
        def body(i, carry):
            convert(*where(i))
            return carry

        lax.fori_loop(0, n, body, 0)

    lhs = ((ch, cl), (xh, xl), (xh, xl))
    w_rows = [pl.ds(pl.multiple_of(lax.rem(j + NZH - zh, NZH) * 32, 32), 32) for j in range(NZH)]

    def forward(bs, k, first=False):
        wh, wl = split(jnp.concatenate([w[b, k, r, :] for b in bs for r in w_rows], axis=0))
        ah, al = lhs[k]
        if len(bs) == 2:
            h = jnp.concatenate([ah[b] for b in bs], axis=1)
            l = jnp.concatenate([al[b] for b in bs], axis=1)
        else:
            h, l = ah[bs[0]], al[bs[0]]
        v = dot3(h, l, wh, wl)
        if first:
            acc[k] = v
        else:
            acc[k] += v

    w_own(2)
    w_own(0)
    w_own(1)
    for j in range(2):
        own_to(0, j, xs[0], a_recv.at[3, 0, j])
        own_to(2, j, xs[1], a_recv.at[1, 0, j])
    w_first(0)
    w_first(1)
    for j in range(2):
        own_to(4, j, zpart, a_recv.at[0, 1, j])
    for j in range(2):
        remote(rows_src[j], xc.at[own, c, j], 0, s_recv.at[0, 0], sib)
        local_copy(rows_src[j], xc.at[own, c, j], own_sem)

    wait(part(U, y, None), o_recv.at[1])
    y_start(U, 1)
    z_start(0)
    wait(part(A, y, None), o_recv.at[0])
    y_start(A, 1)
    y_next(U, 1)
    z_start(1)
    z_start(7)
    y_next(A, 1)
    y_next(U, 2)
    z_start(2)
    z_start(6)
    from_left(0)
    wait(part(B0, y, None), w_recv.at[0])
    y_start(B0, 1)
    from_right(0)
    a_end(1, 0, 0)
    to_sibling(1, 0)
    a_end(3, 0, 1)
    to_sibling(3, 0)
    y_next(A, 2)
    y_next(U, 3)
    z_start(3)
    z_start(5)
    wait(part(B1, y, None), w_recv.at[1])
    y_start(B1, 1)
    y_next(B0, 1)
    a_end(0, 1, 0)
    pass_on(6, 0, 1, 0, 0, 3)
    pass_on(8, 0, 1, 0, 1, 1)
    for j in range(2):
        a_end(2, 0, j)
    to_sibling(2, 0)
    y_next(A, 3)
    y_end(U, 4)
    z_start(4)
    y_next(B1, 1)
    a_end(0, 1, 1)
    pass_on(9, 0, 1, 1, 1, 1)
    pass_on(7, 0, 1, 1, 0, 3)
    to_sibling(0, 1)
    y_next(B0, 2)
    wait(xc.at[own, c], own_sem)
    s_end(0, 0)
    s_end(1, 0)
    s_end(3, 0)
    convert_many(6, lambda i: (lax.rem(x + 3 + i // 2, NX) * NZL + zl, lax.rem(i, 2)))
    from_left(1)
    z_relay(0)
    z_relay(1)
    z_relay(7)
    y_next(B1, 2)
    s_end(2, 0)
    convert_many(2, lambda i: (lax.rem(x + 2, NX) * NZL + zl, i))
    s_end(0, 1)
    convert_many(2, lambda i: (x * NZL + 1 - zl, i))
    from_right(1)
    a_end(1, 1, 0)
    to_sibling(1, 1)
    a_end(3, 1, 1)
    to_sibling(3, 1)
    y_next(B0, 3)
    z_relay(2)
    z_relay(6)
    z_relay(3)
    z_relay(5)
    a_end(2, 1, 0)
    y_next(B1, 3)
    a_end(2, 1, 1)
    to_sibling(2, 1)
    z_relay(4)
    s_end(1, 1)
    s_end(3, 1)
    convert_many(4, lambda i: (lax.rem(x + 3 + 2 * (i // 2), NX) * NZL + 1 - zl, lax.rem(i, 2)))
    s_end(2, 1)
    convert_many(2, lambda i: (lax.rem(x + 2, NX) * NZL + 1 - zl, i))
    pairs = [(y_of(d), y_of(8 - d)) for d in range(1, 4)] + [(y, y_of(4))]
    for k in range(2):
        for i in range(3):
            forward(pairs[i], k, i == 0)
    y_end(A, 4)
    y_end(B0, 4)
    y_end(B1, 4)
    for k in range(2):
        forward(pairs[3], k)

    def grad_rows(m):
        def body(r, carry):
            rows = pl.ds(pl.multiple_of(r * 64, 64), 64)
            gate = acc[1, rows, :]
            s = 1.0 / (1.0 + jnp.exp(-gate))
            bs = acc[0, rows, :] * s
            v = bs * gate if m == 1 else bs * acc[2, rows, :] * (1.0 + gate * (1.0 - s))
            hi, lo = split(v)
            rh[m, rows, :] = hi
            rl[m, rows, :] = lo
            return carry

        lax.fori_loop(0, 8, body, 0)

    def backward(bs, m):
        h = jnp.concatenate([xth[b] for b in bs], axis=0) if len(bs) == 2 else xth[bs[0]]
        l = jnp.concatenate([xtl[b] for b in bs], axis=0) if len(bs) == 2 else xtl[bs[0]]
        v = dot3(h, l, rh[m], rl[m])
        for i, b in enumerate(bs):
            rows = slice(i * 128, i * 128 + 128)
            gbuf[b, 2 * m] = v[rows, 0:128]
            if m == 0:
                gbuf[b, 1] = v[rows, 128:256]
            else:
                gz[b] = v[rows, 128:256]

    def r_start(s, q, d):
        b = y_of(5 - s) if d == 0 else y_of(3 + s)
        rows = pl.ds(64 * d, 64) if s == 1 else pl.ds(0, 128)
        remote(
            gbuf.at[b, q, rows, :], rbuf.at[d, s - 1, q, rows, :],
            2, r_recv.at[s - 1, q], ys[d],
        )

    def r_step(s, *qs):
        for q in qs:
            if s > 1:
                wait_rows(128 if s == 2 else 256, r_recv.at[s - 2, q])
            for d in range(2):
                b = y_of(5 - s) if d == 0 else y_of(3 + s)
                rows = pl.ds(64 * d, 64) if s == 2 else pl.ds(0, 128)
                if s > 1:
                    gbuf[b, q, rows, :] += rbuf[d, s - 2, q, rows, :]
                r_start(s, q, d)

    def r_end(q):
        wait_rows(256, r_recv.at[3, q])
        for i in range(8):
            rows = pl.ds(16 * i, 16)
            tbuf[q, i] = gbuf[y, q, rows, :] + rbuf[0, 3, q, rows, :] + rbuf[1, 3, q, rows, :]
        src = zh * 2 + c
        for dz, dc in zpeers + [(0, 1)]:
            remote(
                tbuf.at[q, zat[dz] * 2 + core_of(dc)], zbuf.at[q, src],
                2, z_recv.at[q], dev_of(0, dz, dc),
            )
        zbuf[q, src] = tbuf[q, src]

    def z_rows(d, first, n):
        return pl.ds(pl.multiple_of(zat[d] * 32 + first, 16), n)

    grad_rows(1)
    backward((y_of(4),), 1)
    r_step(1, 2)
    for i in range(3):
        z_end(i + 1)
        z_end(7 - i)
    for i in range(3):
        forward(pairs[i], 2, i == 0)
    z_end(0)
    z_end(4)
    forward(pairs[3], 2)
    grad_rows(0)
    backward((y_of(4),), 0)
    r_step(1, 0, 1)
    for i in (2, 1, 0):
        backward(pairs[i], 1)
    backward((y,), 1)
    for d in range(2):
        remote(gz.at[:, z_rows(2, 16 * d, 16), :], rz1.at[d], 2, f_recv.at[0, d], zs[d])
    r_step(2, 2)
    backward(pairs[2], 0)
    r_step(2, 0, 1)
    r_step(3, 2)
    for d, dz in ((0, 1), (1, 3)):
        wait(rz1.at[d], f_recv.at[0, d])
        rows = z_rows(dz, 16 * d, 16)
        gz[:, rows, :] = gz[:, rows, :] + rz1[d]
        remote(gz.at[:, z_rows(dz, 0, 32), :], rz2.at[d], 2, f_recv.at[1, d], zs[d])
    backward(pairs[1], 0)
    r_step(3, 0, 1)
    backward(pairs[0], 0)
    r_step(4, 2)
    r_step(4, 0, 1)
    backward((y,), 0)
    r_end(2)
    for d in range(2):
        wait(rz2.at[d], f_recv.at[1, d])
    rows = z_rows(0, 0, 32)
    gz[:, rows, :] = gz[:, rows, :] + rz2[0] + rz2[1]
    for dy, dc in ypeers + [(0, 1)]:
        rows = pl.ds(pl.multiple_of(zh * 32 + core_of(dc) * 16, 16), 16)
        remote(gz.at[y_of(dy), rows, :], yz.at[y * 2 + c], 2, g_recv, dev_of(dy, 0, dc))
    yz[y * 2 + c] = gz[y, pl.ds(pl.multiple_of(zh * 32 + c * 16, 16), 16), :]
    r_end(0)
    r_end(1)
    wait(yz.at[pl.ds(0, 15)], g_recv)
    for cc in range(2):
        v = yz[cc]
        for i in range(1, NY):
            v = v + yz[2 * i + cc]
        out_ref[1, :, cc * 256 + 128 : cc * 256 + 256] = v
    for q in (2, 0, 1):
        wait(zbuf.at[q, pl.ds(0, 7)], z_recv.at[q])
        for cc in range(2):
            col = cc * 256 + (q % 2) * 128
            out_ref[q // 2, :, col : col + 128] = (
                (zbuf[q, cc] + zbuf[q, 2 + cc]) + (zbuf[q, 4 + cc] + zbuf[q, 6 + cc])
            )

    for group in range(3):
        wait(counted.at[pl.ds(0, sent_rows[group]), :], sent.at[group])


def grads(inputs, cotangent, gate_weight, up_weight, down_weight):
    dma = pltpu.SemaphoreType.DMA
    return pl.pallas_call(
        kernel,
        name="grads",
        out_shape=jax.ShapeDtypeStruct((2, 16, 512), F32),
        in_specs=[pl.BlockSpec(memory_space=pl.ANY)] * 5,
        out_specs=pl.BlockSpec(memory_space=pltpu.VMEM),
        scratch_shapes=[
            pltpu.VMEM((8, 2, 2, 256, 128), F32),
            pltpu.VMEM((8, 3, 128, 256), F32),
            pltpu.VMEM((8, 512, 128), BF16),
            pltpu.VMEM((8, 512, 128), BF16),
            pltpu.VMEM((8, 512, 128), BF16),
            pltpu.VMEM((8, 512, 128), BF16),
            pltpu.VMEM((8, 128, 512), BF16),
            pltpu.VMEM((8, 128, 512), BF16),
            pltpu.VMEM((3, 512, 256), F32),
            pltpu.VMEM((2, 512, 256), BF16),
            pltpu.VMEM((2, 512, 256), BF16),
            pltpu.VMEM((8, 3, 128, 128), F32),
            pltpu.VMEM((2, 4, 3, 128, 128), F32),
            pltpu.VMEM((3, 8, 16, 128), F32),
            pltpu.VMEM((3, 8, 16, 128), F32),
            pltpu.VMEM((8, 128, 128), F32),
            pltpu.VMEM((2, 8, 16, 128), F32),
            pltpu.VMEM((2, 8, 32, 128), F32),
            pltpu.VMEM((16, 16, 128), F32),
            pltpu.VMEM((8192, 128), F32),
            dma((3,)),
            dma,
            dma((4, 2, 2)),
            dma((4, 2)),
            dma((2,)),
            dma((2,)),
            dma((4, 4)),
            dma((2, 8)),
            dma((4, 3)),
            dma((3,)),
            dma((2, 2)),
            dma,
        ],
        compiler_params=pltpu.CompilerParams(
            collective_id=0, has_side_effects=True, vmem_limit_bytes=66400000
        ),
    )(inputs, cotangent, gate_weight, up_weight, down_weight)


def local(
    inputs,
    cotangent,
    gate_weight,
    up_weight,
    down_weight,
    gate_first,
    gate_second,
    up_first,
    up_second,
):
    g = grads(inputs, cotangent, gate_weight, up_weight, down_weight)
    gate_new, gate_first_new, gate_second_new = adam_update(
        gate_weight, gate_first, gate_second, g[0]
    )
    up_new, up_first_new, up_second_new = adam_update(up_weight, up_first, up_second, g[1])
    return (gate_new, gate_first_new, gate_second_new, up_new, up_first_new, up_second_new)


def solution(mesh):
    spec = P("dp", "tensor")
    return jax.shard_map(
        local, mesh=mesh, in_specs=(spec,) * 9, out_specs=(spec,) * 6, check_vma=False
    )
```

```python
import jax
import jax.numpy as jnp
from jax import lax
from jax.experimental import pallas as pl
from jax.experimental.pallas import tpu as pltpu
from jax.sharding import PartitionSpec as P

STEP = 100
MESH = pl.DeviceIdType.MESH
F32 = jnp.float32
BF16 = jnp.bfloat16
NX, NZL, NY, NZH = 4, 2, 8, 4


def adam_update(weight, first, second, grad):
    first_new = 0.9 * first + 0.1 * grad
    second_new = 0.95 * second + 0.05 * grad * grad
    first_hat = first_new / (1.0 - 0.9**STEP)
    second_hat = second_new / (1.0 - 0.95**STEP)
    weight_new = weight - 0.003 * first_hat / (jnp.sqrt(second_hat) + 1e-08)
    return (weight_new, first_new, second_new)


def split(v):
    hi = v.astype(BF16)
    return hi, (v - hi.astype(F32)).astype(BF16)


def dot(a, b):
    return jnp.dot(a, b, preferred_element_type=F32)


def dot3(ah, al, bh, bl):
    return dot(ah, bh) + dot(ah, bl) + dot(al, bh)


def kernel(
    in_ref, cot_ref, gw_ref, uw_ref, dw_ref, out_ref,
    xc, w, xh, xl, ch, cl, xth, xtl, acc, rh, rl,
    gbuf, rbuf, tbuf, zbuf, gz, rz1, rz2, yz,
    counted, sent, own_sem, a_recv, s_recv, o_recv, w_recv, y_recv, u_recv, r_recv, z_recv, f_recv, g_recv,
):
    dp = lax.axis_index("dp")
    t = lax.axis_index("tensor")
    c = lax.rem(dp, 2)
    zh = lax.rem(dp // 2, NZH)
    y = dp // (2 * NZH)
    x = t // NZL
    zl = lax.rem(t, NZL)

    def t_of(dx, dz):
        zz = zl if dz == 0 else 1 - zl
        return lax.rem(x + dx, NX) * NZL + zz

    def y_of(d):
        return lax.rem(y + d, NY)

    def core_of(dc):
        return c if dc == 0 else 1 - c

    def dev_of(dy, dz, dc):
        return ((y_of(dy) * NZH + zat[dz]) * 2 + core_of(dc), t)

    zat = [lax.rem(zh + d, NZH) for d in range(NZH)]
    sib = dev_of(0, 0, 1)
    zpart = (dp, t_of(0, 1))
    xs = ((dp, t_of(1, 0)), (dp, t_of(3, 0)))
    ys = (dev_of(1, 0, 0), dev_of(7, 0, 0))
    zs = (dev_of(0, 1, 0), dev_of(0, 3, 0))
    zpeers = [(2, 0), (2, 1), (1, 0), (3, 0), (1, 1), (3, 1)]
    ypeers = [(dy, dc) for dy in (4, 3, 5, 2, 6, 1, 7) for dc in range(2)]

    barrier = pltpu.get_barrier_semaphore()
    peers = [dev_of(0, dz, dc) for dz, dc in zpeers] + [sib, zpart, xs[0], xs[1]]
    peers = peers + [dev_of(dy, 0, dc) for dy, dc in ypeers]
    for peer in peers:
        pl.semaphore_signal(barrier, inc=1, device_id=peer, device_id_type=MESH)
    pl.semaphore_wait(barrier, len(peers))

    sent_rows = [0, 0, 0]

    def remote(src, dst, group, recv, dev):
        n = 1
        for extent in src.shape:
            n = n * extent
        sent_rows[group] += n // 128
        pltpu.make_async_remote_copy(
            src_ref=src, dst_ref=dst, send_sem=sent.at[group], recv_sem=recv,
            device_id=dev, device_id_type=MESH,
        ).start()

    def local_copy(src, dst, sem):
        pltpu.make_async_copy(src, dst, sem).start()

    def wait(ref, sem):
        pltpu.make_async_copy(ref, ref, sem).wait()

    def wait_rows(n, sem):
        wait(counted.at[pl.ds(0, n), :], sem)

    w_srcs = (dw_ref, gw_ref, uw_ref)

    def w_own(k):
        mine = pl.ds(pl.multiple_of(c * 16, 16), 16)
        there = pl.ds(pl.multiple_of((1 - c) * 256, 256), 256)
        remote(w_srcs[k].at[:, there], w.at[y, k, mine, :], 1, o_recv.at[k // 2], sib)
        here = pl.ds(pl.multiple_of(c * 256, 256), 256)
        local_copy(w_srcs[k].at[:, here], w.at[y, k, mine, :], o_recv.at[k // 2])

    def w_first(k):
        for dz, dc in zpeers:
            src = w_srcs[k].at[:, pl.ds(pl.multiple_of(core_of(dc) * 256, 256), 256)]
            rows = pl.ds(pl.multiple_of((4 - dz) * 32 + c * 16, 16), 16)
            remote(src, w.at[y, k, rows, :], 1, w_recv.at[k], dev_of(0, dz, dc))

    U, A, B0, B1 = range(4)

    def part(ring, b, half):
        if ring == A:
            return w.at[b, pl.ds(0, 2), pl.ds(0, 32), :] if half is None else w.at[b, half, pl.ds(0, 32), :]
        k = (2, 0, 0, 1)[ring]
        first, n = (0, 32) if ring == U else (32, 96)
        if half is not None:
            n = n // 2
            first = first + half * n
        return w.at[b, k, pl.ds(first, n), :]

    def step_parts(ring, s, back):
        if s < 4:
            return part(ring, y_of((9 - s - back) % 8), None), part(ring, y_of(s - 1 + back), None)
        return part(ring, y_of(5 - back), 0), part(ring, y_of(3 + back), 1)

    def y_start(ring, s):
        for d, r in enumerate(step_parts(ring, s, 0)):
            remote(r, r, 1, y_recv.at[s - 1, ring], ys[d])

    def y_end(ring, s):
        wait_rows((128, 256, 384, 384)[ring] // (2 if s == 4 else 1), y_recv.at[s - 1, ring])

    def y_next(ring, s):
        y_end(ring, s)
        y_start(ring, s + 1)

    def z_start(i):
        b = y_of(i)
        for d, first in enumerate((96, 32)):
            remote(w.at[b, 2, pl.ds(0, 32), :], w.at[b, 2, pl.ds(first, 32), :], 1, u_recv.at[0, i], zs[d])

    def z_relay(i):
        b = y_of(i)
        wait_rows(128, u_recv.at[0, i])
        for d, (src, dst) in enumerate(((96, 64), (48, 80))):
            remote(w.at[b, 2, pl.ds(src, 16), :], w.at[b, 2, pl.ds(dst, 16), :], 1, u_recv.at[1, i], zs[d])

    def z_end(i):
        wait_rows(64, u_recv.at[1, i])

    own = t_of(0, 0)
    rows_src = (in_ref, cot_ref)

    def own_to(n, j, dev, recv):
        remote(rows_src[j], xc.at[own, c, j], 0, recv, dev)

    def pass_on(n, dx, dz, j, d, to_dx):
        b = xc.at[t_of(dx, dz), c, j]
        remote(b, b, 0, a_recv.at[to_dx, dz, j], xs[d])

    def a_end(dx, dz, j):
        wait(xc.at[t_of(dx, dz), c, j], a_recv.at[dx, dz, j])

    def from_right(dz):
        a_end(1, dz, 1)
        pass_on(10 + dz, 1, dz, 1, 1, 2)

    def from_left(dz):
        a_end(3, dz, 0)
        pass_on(12 + dz, 3, dz, 0, 0, 2)

    def to_sibling(dx, dz):
        b = xc.at[t_of(dx, dz), c]
        remote(b, b, 0, s_recv.at[dx, dz], sib)

    def s_end(dx, dz):
        wait(xc.at[t_of(dx, dz), 1 - c], s_recv.at[dx, dz])

    def convert(tt, cc):
        rows = pl.ds(pl.multiple_of(cc * 256, 256), 256)
        v = xc[tt, cc, 0]
        hi, lo = split(v)
        xh[tt, rows, :] = hi
        xl[tt, rows, :] = lo
        hi, lo = split(jnp.transpose(v))
        xth[tt, :, rows] = hi
        xtl[tt, :, rows] = lo
        hi, lo = split(xc[tt, cc, 1])
        ch[tt, rows, :] = hi
        cl[tt, rows, :] = lo

    def convert_many(n, where):
        def body(i, carry):
            convert(*where(i))
            return carry

        lax.fori_loop(0, n, body, 0)

    lhs = ((ch, cl), (xh, xl), (xh, xl))
    w_rows = [pl.ds(pl.multiple_of(lax.rem(j + NZH - zh, NZH) * 32, 32), 32) for j in range(NZH)]

    def forward(bs, k, first=False):
        wh, wl = split(jnp.concatenate([w[b, k, r, :] for b in bs for r in w_rows], axis=0))
        ah, al = lhs[k]
        if len(bs) == 2:
            h = jnp.concatenate([ah[b] for b in bs], axis=1)
            l = jnp.concatenate([al[b] for b in bs], axis=1)
        else:
            h, l = ah[bs[0]], al[bs[0]]
        v = dot3(h, l, wh, wl)
        if first:
            acc[k] = v
        else:
            acc[k] += v

    w_own(2)
    w_own(0)
    w_own(1)
    for j in range(2):
        own_to(0, j, xs[0], a_recv.at[3, 0, j])
        own_to(2, j, xs[1], a_recv.at[1, 0, j])
    w_first(0)
    w_first(1)
    for j in range(2):
        own_to(4, j, zpart, a_recv.at[0, 1, j])
    for j in range(2):
        remote(rows_src[j], xc.at[own, c, j], 0, s_recv.at[0, 0], sib)
        local_copy(rows_src[j], xc.at[own, c, j], own_sem)

    wait(part(U, y, None), o_recv.at[1])
    y_start(U, 1)
    wait(part(A, y, None), o_recv.at[0])
    y_start(A, 1)
    y_next(U, 1)
    y_next(A, 1)
    y_next(U, 2)
    from_left(0)
    wait(part(B0, y, None), w_recv.at[0])
    y_start(B0, 1)
    from_right(0)
    a_end(1, 0, 0)
    to_sibling(1, 0)
    a_end(3, 0, 1)
    to_sibling(3, 0)
    y_next(A, 2)
    y_next(U, 3)
    wait(part(B1, y, None), w_recv.at[1])
    y_start(B1, 1)
    for i in (0, 1, 7, 2, 6, 3, 5):
        z_start(i)
    y_next(B0, 1)
    a_end(0, 1, 0)
    pass_on(6, 0, 1, 0, 0, 3)
    pass_on(8, 0, 1, 0, 1, 1)
    for j in range(2):
        a_end(2, 0, j)
    to_sibling(2, 0)
    y_next(A, 3)
    y_end(U, 4)
    z_start(4)
    y_next(B1, 1)
    a_end(0, 1, 1)
    pass_on(9, 0, 1, 1, 1, 1)
    pass_on(7, 0, 1, 1, 0, 3)
    to_sibling(0, 1)
    y_next(B0, 2)
    wait(xc.at[own, c], own_sem)
    s_end(0, 0)
    s_end(1, 0)
    s_end(3, 0)
    convert_many(6, lambda i: (lax.rem(x + 3 + i // 2, NX) * NZL + zl, lax.rem(i, 2)))
    from_left(1)
    z_relay(0)
    z_relay(1)
    z_relay(7)
    y_next(B1, 2)
    s_end(2, 0)
    convert_many(2, lambda i: (lax.rem(x + 2, NX) * NZL + zl, i))
    s_end(0, 1)
    convert_many(2, lambda i: (x * NZL + 1 - zl, i))
    from_right(1)
    a_end(1, 1, 0)
    to_sibling(1, 1)
    a_end(3, 1, 1)
    to_sibling(3, 1)
    y_next(B0, 3)
    z_relay(2)
    z_relay(6)
    z_relay(3)
    z_relay(5)
    a_end(2, 1, 0)
    y_next(B1, 3)
    a_end(2, 1, 1)
    to_sibling(2, 1)
    z_relay(4)
    s_end(1, 1)
    s_end(3, 1)
    convert_many(4, lambda i: (lax.rem(x + 3 + 2 * (i // 2), NX) * NZL + 1 - zl, lax.rem(i, 2)))
    s_end(2, 1)
    convert_many(2, lambda i: (lax.rem(x + 2, NX) * NZL + 1 - zl, i))
    pairs = [(y_of(d), y_of(8 - d)) for d in range(1, 4)] + [(y, y_of(4))]
    for k in range(2):
        for i in range(3):
            forward(pairs[i], k, i == 0)
    y_end(A, 4)
    y_end(B0, 4)
    y_end(B1, 4)
    for k in range(2):
        forward(pairs[3], k)

    def grad_rows(m):
        def body(r, carry):
            rows = pl.ds(pl.multiple_of(r * 64, 64), 64)
            gate = acc[1, rows, :]
            s = 1.0 / (1.0 + jnp.exp(-gate))
            bs = acc[0, rows, :] * s
            v = bs * gate if m == 1 else bs * acc[2, rows, :] * (1.0 + gate * (1.0 - s))
            hi, lo = split(v)
            rh[m, rows, :] = hi
            rl[m, rows, :] = lo
            return carry

        lax.fori_loop(0, 8, body, 0)

    def backward(bs, m):
        h = jnp.concatenate([xth[b] for b in bs], axis=0) if len(bs) == 2 else xth[bs[0]]
        l = jnp.concatenate([xtl[b] for b in bs], axis=0) if len(bs) == 2 else xtl[bs[0]]
        v = dot3(h, l, rh[m], rl[m])
        for i, b in enumerate(bs):
            rows = slice(i * 128, i * 128 + 128)
            gbuf[b, 2 * m] = v[rows, 0:128]
            if m == 0:
                gbuf[b, 1] = v[rows, 128:256]
            else:
                gz[b] = v[rows, 128:256]

    def r_start(s, q, d):
        b = y_of(5 - s) if d == 0 else y_of(3 + s)
        rows = pl.ds(64 * d, 64) if s == 1 else pl.ds(0, 128)
        remote(
            gbuf.at[b, q, rows, :], rbuf.at[d, s - 1, q, rows, :],
            2, r_recv.at[s - 1, q], ys[d],
        )

    def r_step(s, *qs):
        for q in qs:
            if s > 1:
                wait_rows(128 if s == 2 else 256, r_recv.at[s - 2, q])
            for d in range(2):
                b = y_of(5 - s) if d == 0 else y_of(3 + s)
                rows = pl.ds(64 * d, 64) if s == 2 else pl.ds(0, 128)
                if s > 1:
                    gbuf[b, q, rows, :] += rbuf[d, s - 2, q, rows, :]
                r_start(s, q, d)

    def r_end(q):
        wait_rows(256, r_recv.at[3, q])
        for i in range(8):
            rows = pl.ds(16 * i, 16)
            tbuf[q, i] = gbuf[y, q, rows, :] + rbuf[0, 3, q, rows, :] + rbuf[1, 3, q, rows, :]
        src = zh * 2 + c
        for dz, dc in zpeers + [(0, 1)]:
            remote(
                tbuf.at[q, zat[dz] * 2 + core_of(dc)], zbuf.at[q, src],
                2, z_recv.at[q], dev_of(0, dz, dc),
            )
        zbuf[q, src] = tbuf[q, src]

    def z_rows(d, first, n):
        return pl.ds(pl.multiple_of(zat[d] * 32 + first, 16), n)

    grad_rows(1)
    backward((y_of(4),), 1)
    r_step(1, 2)
    for i in range(3):
        z_end(i + 1)
        z_end(7 - i)
    for i in range(3):
        forward(pairs[i], 2, i == 0)
    z_end(0)
    z_end(4)
    forward(pairs[3], 2)
    grad_rows(0)
    backward((y_of(4),), 0)
    r_step(1, 0, 1)
    for i in (2, 1, 0):
        backward(pairs[i], 1)
    backward((y,), 1)
    for d in range(2):
        remote(gz.at[:, z_rows(2, 16 * d, 16), :], rz1.at[d], 2, f_recv.at[0, d], zs[d])
    r_step(2, 2)
    backward(pairs[2], 0)
    r_step(2, 0, 1)
    r_step(3, 2)
    for d, dz in ((0, 1), (1, 3)):
        wait(rz1.at[d], f_recv.at[0, d])
        rows = z_rows(dz, 16 * d, 16)
        gz[:, rows, :] = gz[:, rows, :] + rz1[d]
        remote(gz.at[:, z_rows(dz, 0, 32), :], rz2.at[d], 2, f_recv.at[1, d], zs[d])
    backward(pairs[1], 0)
    r_step(3, 0, 1)
    backward(pairs[0], 0)
    r_step(4, 2)
    r_step(4, 0, 1)
    backward((y,), 0)
    r_end(2)
    for d in range(2):
        wait(rz2.at[d], f_recv.at[1, d])
    rows = z_rows(0, 0, 32)
    gz[:, rows, :] = gz[:, rows, :] + rz2[0] + rz2[1]
    for dy, dc in ypeers + [(0, 1)]:
        rows = pl.ds(pl.multiple_of(zh * 32 + core_of(dc) * 16, 16), 16)
        remote(gz.at[y_of(dy), rows, :], yz.at[y * 2 + c], 2, g_recv, dev_of(dy, 0, dc))
    yz[y * 2 + c] = gz[y, pl.ds(pl.multiple_of(zh * 32 + c * 16, 16), 16), :]
    r_end(0)
    r_end(1)
    wait(yz.at[pl.ds(0, 15)], g_recv)
    for cc in range(2):
        v = yz[cc]
        for i in range(1, NY):
            v = v + yz[2 * i + cc]
        out_ref[1, :, cc * 256 + 128 : cc * 256 + 256] = v
    for q in (2, 0, 1):
        wait(zbuf.at[q, pl.ds(0, 7)], z_recv.at[q])
        for cc in range(2):
            col = cc * 256 + (q % 2) * 128
            out_ref[q // 2, :, col : col + 128] = (
                (zbuf[q, cc] + zbuf[q, 2 + cc]) + (zbuf[q, 4 + cc] + zbuf[q, 6 + cc])
            )

    for group in range(3):
        wait(counted.at[pl.ds(0, sent_rows[group]), :], sent.at[group])


def grads(inputs, cotangent, gate_weight, up_weight, down_weight):
    dma = pltpu.SemaphoreType.DMA
    return pl.pallas_call(
        kernel,
        name="grads",
        out_shape=jax.ShapeDtypeStruct((2, 16, 512), F32),
        in_specs=[pl.BlockSpec(memory_space=pl.ANY)] * 5,
        out_specs=pl.BlockSpec(memory_space=pltpu.VMEM),
        scratch_shapes=[
            pltpu.VMEM((8, 2, 2, 256, 128), F32),
            pltpu.VMEM((8, 3, 128, 256), F32),
            pltpu.VMEM((8, 512, 128), BF16),
            pltpu.VMEM((8, 512, 128), BF16),
            pltpu.VMEM((8, 512, 128), BF16),
            pltpu.VMEM((8, 512, 128), BF16),
            pltpu.VMEM((8, 128, 512), BF16),
            pltpu.VMEM((8, 128, 512), BF16),
            pltpu.VMEM((3, 512, 256), F32),
            pltpu.VMEM((2, 512, 256), BF16),
            pltpu.VMEM((2, 512, 256), BF16),
            pltpu.VMEM((8, 3, 128, 128), F32),
            pltpu.VMEM((2, 4, 3, 128, 128), F32),
            pltpu.VMEM((3, 8, 16, 128), F32),
            pltpu.VMEM((3, 8, 16, 128), F32),
            pltpu.VMEM((8, 128, 128), F32),
            pltpu.VMEM((2, 8, 16, 128), F32),
            pltpu.VMEM((2, 8, 32, 128), F32),
            pltpu.VMEM((16, 16, 128), F32),
            pltpu.VMEM((8192, 128), F32),
            dma((3,)),
            dma,
            dma((4, 2, 2)),
            dma((4, 2)),
            dma((2,)),
            dma((2,)),
            dma((4, 4)),
            dma((2, 8)),
            dma((4, 3)),
            dma((3,)),
            dma((2, 2)),
            dma,
        ],
        compiler_params=pltpu.CompilerParams(
            collective_id=0, has_side_effects=True, vmem_limit_bytes=66400000
        ),
    )(inputs, cotangent, gate_weight, up_weight, down_weight)


def local(
    inputs,
    cotangent,
    gate_weight,
    up_weight,
    down_weight,
    gate_first,
    gate_second,
    up_first,
    up_second,
):
    g = grads(inputs, cotangent, gate_weight, up_weight, down_weight)
    gate_new, gate_first_new, gate_second_new = adam_update(
        gate_weight, gate_first, gate_second, g[0]
    )
    up_new, up_first_new, up_second_new = adam_update(up_weight, up_first, up_second, g[1])
    return (gate_new, gate_first_new, gate_second_new, up_new, up_first_new, up_second_new)


def solution(mesh):
    spec = P("dp", "tensor")
    return jax.shard_map(
        local, mesh=mesh, in_specs=(spec,) * 9, out_specs=(spec,) * 6, check_vma=False
    )
```
